256 devices in a mesh: sect: 16 (over x, y), sec: 16 (over z, core).
Axes of the slice: x: 4, y: 4, z: 8, core: 2. Of those that a mesh axis runs over, the one named last changes fastest.
Arguments:
- psi_first: bfloat16 [16, 128, 128, 128], P('sect', 'sec'), may hold values from -100 to 100
- psi_second: bfloat16 [16, 128, 128, 128], P('sect', 'sec'), may hold values from -100 to 100
- left_env: bfloat16 [16, 14, 128, 128, 128], P('sect', None, 'sec'), may hold values from -1 to 2
- right_env: bfloat16 [16, 14, 128, 128, 128], P('sect', None, 'sec'), may hold values from -1 to 2
- couplings: float32 [16, 128, 4, 14], P('sect', 'sec'), may hold values from -2 to 3
- pair_sector: int32 [128, 4], P('sec'), may hold values from 0 to 127, as said below
Outputs:
- wave_first: bfloat16 [16, 128, 128, 128], P('sect', 'sec')
- wave_second: bfloat16 [16, 128, 128, 128], P('sect', 'sec')
- energies: float32 [16, 2], P('sect')
The draws below stay inside these ranges and needn't reach their ends.
Inputs may be any that keep to these rules, and one draw needn't show every extreme that they name: `pair_sector`: A sector held at local position l of index d of sec (sector d * 8 + l) names only sectors o * 8 + ((d + k) mod 8) with 0 <= k < 2, for any o.
All inputs are finite; a program needn't handle non-finite values.
Results may differ from the reference program's by a relative error of at most 0.035.
Values may be sent and summed in bfloat16 or wider, within the bound.
A program may use at most 128 MiB of HBM per device.

```python
import jax
import jax.numpy as jnp
from jax import lax

BLK = 128
MPO = 14
SEC_DEV = 8
PAIRS = 4
MOST = 2
ITERS = 3
SECTORS = 128
N_SECT = 16


def wave_draw(key):
    shape = (N_SECT, SECTORS, BLK, BLK)
    keys = jax.random.split(key, 6)
    rows = 10.0 ** jax.random.uniform(keys[1], (N_SECT, SECTORS, BLK, 1), jnp.float32)
    cols = 10.0 ** jax.random.uniform(keys[2], (N_SECT, SECTORS, 1, BLK), jnp.float32)
    common_rows = 10.0 ** jax.random.uniform(keys[4], (N_SECT, 1, BLK, 1), jnp.float32)
    common_cols = 10.0 ** jax.random.uniform(keys[5], (N_SECT, 1, 1, BLK), jnp.float32)
    ramp = 1.0 + 2.0 * jnp.arange(SECTORS, dtype=jnp.float32) / max(SECTORS - 1, 1)
    base = jax.random.normal(keys[0], shape, jnp.float32)
    shared = jax.random.normal(keys[3], (N_SECT, 1, BLK, BLK), jnp.float32)
    mixture = base * rows * cols + shared * common_rows * common_cols
    values = mixture * ramp[None, :, None, None] / 12.0
    return jnp.clip(values, -100.0, 100.0).astype(jnp.bfloat16)


def draw_psi_first(key, part):
    return wave_draw(jax.random.fold_in(key, 11))


def draw_psi_second(key, part):
    return wave_draw(jax.random.fold_in(key, 23))


def env_draw(key):
    identity = jnp.eye(BLK, dtype=jnp.float32)
    scale = BLK ** (-0.5)

    def one_section(index):
        sub = jax.random.fold_in(key, index)
        keys = jax.random.split(sub, 2)
        shape = (MPO, SECTORS, BLK, BLK)
        off = jnp.clip(jax.random.normal(keys[0], shape, jnp.float32), -4.0, 4.0) * scale
        diag = jax.random.uniform(keys[1], (MPO, SECTORS, 1, 1), jnp.float32, 0.6, 1.0)
        return (off + diag * identity).astype(jnp.bfloat16)
    return lax.map(one_section, jnp.arange(N_SECT, dtype=jnp.int32))


def draw_left_env(key, part):
    return env_draw(jax.random.fold_in(key, 41))


def draw_right_env(key, part):
    return env_draw(jax.random.fold_in(key, 53))


def draw_couplings(key, part):
    sub = jax.random.fold_in(key, 67)
    shape = (N_SECT, SECTORS, PAIRS, MPO)
    spread = jnp.clip(0.5 * jax.random.normal(sub, shape, jnp.float32), -1.5, 1.5)
    lift = jnp.where(jnp.arange(MPO, dtype=jnp.int32) == 0, 1.5, 0.0).astype(jnp.float32)
    return spread + lift[None, None, None, :]


def draw_pair_sector(key, part):
    keys = jax.random.split(jax.random.fold_in(key, 37), 2)
    owners_n = SECTORS // SEC_DEV
    owners = jax.random.randint(keys[0], (SECTORS, PAIRS), 0, owners_n)
    owners = owners.at[:, 1].set(owners[:, 0])
    shifts = jax.random.randint(keys[1], (SECTORS, PAIRS), 0, MOST)
    shifts = shifts.at[:, 0].set(0).at[:, 1].set(1)
    holder = (jnp.arange(SECTORS, dtype=jnp.int32) // SEC_DEV)[:, None]
    local = (holder + shifts) % SEC_DEV
    return (owners * SEC_DEV + local).astype(jnp.int32)


def setup_inputs(seed: int = 0) -> dict:
    key_of = jax.random.split(jax.random.key(seed), 7)
    return {
        "psi_first": draw_psi_first(jax.random.fold_in(key_of[6], 71), 0),
        "psi_second": draw_psi_second(jax.random.fold_in(key_of[6], 71), 0),
        "left_env": draw_left_env(jax.random.fold_in(key_of[6], 71), 0),
        "right_env": draw_right_env(jax.random.fold_in(key_of[6], 71), 0),
        "couplings": draw_couplings(jax.random.fold_in(key_of[6], 71), 0),
        "pair_sector": draw_pair_sector(jax.random.fold_in(key_of[6], 71), 0),
    }


def hamiltonian(wave_b, left, right, coup, pairs):
    blocks = wave_b.astype(jnp.float32)[pairs]
    mixed = jnp.einsum('sjm,sjab->msab', coup, blocks).astype(jnp.bfloat16)
    inner = jnp.einsum('msab,msbc->msac', left.astype(jnp.float32), mixed.astype(jnp.float32)).astype(jnp.bfloat16)
    return jnp.einsum('msab,msbc->sac', inner.astype(jnp.float32), right.astype(jnp.float32))

def bond_step(start, left, right, coup, pairs):
    state = start.astype(jnp.float32)
    total = state.shape[0] * state.shape[1] * state.shape[2]
    quot = jnp.float32(0.0)
    for step in range(ITERS):
        wave_b = state.astype(jnp.bfloat16)
        image = hamiltonian(wave_b, left, right, coup, pairs)
        flat = wave_b.astype(jnp.float32)
        norm_sq = jnp.sum(flat * flat)
        numer = jnp.sum(flat * image)
        quot = numer / norm_sq
        fresh = flat - 0.1 * (image - quot * flat)
        size_sq = jnp.sum(fresh * fresh)
        state = fresh * lax.rsqrt(size_sq / total)
    return (state.astype(jnp.bfloat16), quot)

def transport(wave_b, left):
    transit = jnp.einsum('msab,sbc->msac', left.astype(jnp.float32), wave_b.astype(jnp.float32)).astype(jnp.bfloat16)
    passed = jnp.einsum('sba,msbc->msac', wave_b.astype(jnp.float32), transit.astype(jnp.float32))
    return (passed / BLK).astype(jnp.bfloat16)

def reference(psi_first, psi_second, left_env, right_env, couplings, pair_sector):
    firsts, seconds, energy_rows = ([], [], [])
    carried = None
    for section in range(N_SECT):
        wave_one, quot_one = bond_step(psi_first[section], left_env[section], right_env[section], couplings[section], pair_sector)
        used = left_env[section] if section == 0 else carried
        wave_two, quot_two = bond_step(psi_second[section], used, right_env[section], couplings[section], pair_sector)
        carried = transport(wave_one, left_env[section])
        firsts.append(wave_one)
        seconds.append(wave_two)
        energy_rows.append(jnp.stack([quot_one, quot_two]))
    return (jnp.stack(firsts), jnp.stack(seconds), jnp.stack(energy_rows))
```

```python
import functools

import jax
import jax.numpy as jnp
from jax import lax
from jax.experimental import pallas as pl
from jax.experimental.pallas import tpu as pltpu
from jax.sharding import PartitionSpec as P

MESH = pl.DeviceIdType.MESH
BLK = 128
ITERS = 3
DESCENT = 0.1
F32 = jnp.float32
BF16 = jnp.bfloat16


def fold(tile):
    return jnp.sum(tile.reshape(tile.shape[0] // 8, 8, tile.shape[1]), axis=0)


def kernel(
    n_sect,
    n_sec,
    coup,
    pairs,
    psi_one,
    psi_two,
    left,
    right,
    wave_one,
    wave_two,
    energies,
    env,
    renv,
    cand,
    come,
    own,
    sent,
    image,
    stat,
    stat_own,
    coef,
    prev_wave,
    load_sem,
    send_sem,
    recv_sem,
    stat_send,
    stat_recv,
    env_send,
    env_recv,
    hand_sem,
):
    sect = lax.axis_index("sect")
    me = lax.axis_index("sec")
    following = lax.rem(sect + 1, n_sect)
    previous = lax.rem(sect + n_sect - 1, n_sect)
    terms, held = left.shape[0], left.shape[1]
    half = n_sec // 2
    total = float(n_sec * held * BLK * BLK)

    barrier = pltpu.get_barrier_semaphore()

    def greet(step, _):
        peer = lax.rem(me + step, n_sec)
        pl.semaphore_signal(barrier, inc=1, device_id=(sect, peer), device_id_type=MESH)
        return 0

    lax.fori_loop(1, n_sec, greet, 0)
    pl.semaphore_signal(barrier, inc=1, device_id=(following, me), device_id_type=MESH)
    pl.semaphore_signal(barrier, inc=1, device_id=(previous, me), device_id_type=MESH)

    def place(source, target, number):
        return pltpu.make_async_copy(source, target, load_sem.at[number])

    first = lax.rem(me, held)
    second = lax.rem(me + 1, held)
    loads = [
        place(psi_one, own.at[0], 0),
        place(psi_one.at[first], come.at[0, 2 * me], 1),
        place(psi_one.at[second], come.at[0, 2 * me + 1], 2),
        place(left, env.at[0], 3),
        place(right, renv, 4),
        place(psi_two, own.at[1], 5),
        place(psi_two.at[first], come.at[3, 2 * me], 6),
        place(psi_two.at[second], come.at[3, 2 * me + 1], 7),
    ]
    for load in loads:
        load.start()
    pl.semaphore_wait(barrier, n_sec + 1)

    def send_block(source, number, kind, peer):
        pltpu.make_async_remote_copy(
            src_ref=source,
            dst_ref=come.at[number, 2 * me + kind],
            send_sem=send_sem.at[number],
            recv_sem=recv_sem.at[number],
            device_id=(sect, peer),
            device_id_type=MESH,
        ).start()

    def send_sector(source, number, step):
        @pl.when(step != 0)
        def _():
            send_block(source, number, 0, lax.rem(me + step, n_sec))

        send_block(source, number, 0, lax.rem(me + step + half, n_sec))

        @pl.when(step != 1)
        def _():
            send_block(source, number, 1, lax.rem(me + step + n_sec - 1, n_sec))

        send_block(source, number, 1, lax.rem(me + step + half - 1, n_sec))

    def send_start(source, number):
        def body(step, _):
            send_sector(source.at[lax.rem(me + step, held)], number, step)
            return 0

        lax.fori_loop(0, held, body, 0)

    send_start(psi_one, 0)

    def send_env(term, _):
        pltpu.make_async_remote_copy(
            src_ref=left.at[term],
            dst_ref=env.at[1, term],
            send_sem=env_send.at[term],
            recv_sem=env_recv.at[term],
            device_id=(following, me),
            device_id_type=MESH,
        ).start()
        return 0

    lax.fori_loop(0, terms, send_env, 0)

    blocks = pl.ds(0, 2 * n_sec - 2)

    def arrived(number):
        pltpu.make_async_copy(come.at[number, blocks], come.at[number, blocks], recv_sem.at[number]).wait()

    def left_here(number):
        pltpu.make_async_copy(come.at[number, blocks], come.at[number, blocks], send_sem.at[number]).wait()

    for load in loads:
        load.wait()

    def begin(step):
        arrived(3 * step)

        def body(slot, _):
            cand[slot] = come[3 * step, slot]
            return 0

        lax.fori_loop(0, 2 * n_sec, body, 0, unroll=2)
        coef[2] = jnp.zeros((8, BLK), F32)

    def iterate(index, _):
        step = lax.div(index, ITERS)
        turn = lax.rem(index, ITERS)
        number = index + 1

        @pl.when(turn == 0)
        def _():
            begin(step)

        @pl.when(index == ITERS - 1)
        def _():
            send_start(psi_two, 3)

        shift = coef[2, 0:1, :]

        def sector(turned, sums):
            local = lax.rem(me + turned, held)
            slots = []
            for pair in range(4):
                name = pairs[local * 4 + pair]
                slots.append(2 * lax.div(name, held) + lax.rem(name + n_sec - me, held))
            total_image = jnp.zeros((BLK, BLK), F32)
            for term in range(terms):
                mixed = None
                for pair in range(4):
                    part = coup[(local * 4 + pair) * terms + term] * cand[slots[pair]].astype(F32)
                    mixed = part if mixed is None else mixed + part
                inner = jnp.dot(env[step, term, local], mixed.astype(BF16), preferred_element_type=F32)
                total_image = total_image + jnp.dot(
                    inner.astype(BF16), renv[term, local], preferred_element_type=F32
                )
            mine = own[step, local].astype(F32)
            rest = total_image - shift * mine

            @pl.when(turn < ITERS - 1)
            def _():
                sent[index, local] = rest.astype(BF16)

                @pl.when(turned < 2)
                def _():
                    come[number, 2 * me + turned] = rest.astype(BF16)

                send_sector(sent.at[index, local], number, turned)

            @pl.when(turn == ITERS - 1)
            def _():
                image[local] = rest

            square, cross, rests = sums
            return (square + fold(mine * mine), cross + fold(mine * rest), rests + fold(rest * rest))

        zero = jnp.zeros((8, BLK), F32)
        square, cross, rests = lax.fori_loop(0, held, sector, (zero, zero, zero))
        stat_own[index, 0] = square
        stat_own[index, 1] = cross
        stat_own[index, 2] = rests
        stat[index, me] = stat_own[index]

        def tell(offset, _):
            pltpu.make_async_remote_copy(
                src_ref=stat_own.at[index],
                dst_ref=stat.at[index, me],
                send_sem=stat_send.at[index],
                recv_sem=stat_recv.at[index],
                device_id=(sect, lax.rem(me + offset, n_sec)),
                device_id_type=MESH,
            ).start()
            return 0

        lax.fori_loop(1, n_sec, tell, 0)
        others = pl.ds(0, n_sec - 1)
        pltpu.make_async_copy(stat.at[index, others], stat.at[index, others], stat_recv.at[index]).wait()
        sums = [jnp.sum(stat[index, :, kind], axis=0) for kind in range(3)]
        square, cross, rests = [
            jnp.broadcast_to(jnp.sum(value, axis=(0, 1), keepdims=True), (8, BLK)) for value in sums
        ]
        ratio = cross / square
        keep = 1.0 + DESCENT * ratio
        size = keep * keep * square - (2.0 * DESCENT) * keep * cross + (DESCENT * DESCENT) * rests
        scale = lax.rsqrt(size / total)
        coef[0] = keep * scale
        coef[1] = DESCENT * scale
        quot = coef[2] + ratio
        coef[2] = quot

        @pl.when(turn < ITERS - 1)
        def _():
            grow = coef[0, 0:1, :]
            drop = coef[1, 0:1, :]

            def own_body(local, _):
                own[step, local] = (
                    grow * own[step, local].astype(F32) - drop * sent[index, local].astype(F32)
                ).astype(BF16)
                return 0

            lax.fori_loop(0, held, own_body, 0, unroll=2)
            arrived(number)

            def cand_body(slot, _):
                cand[slot] = (
                    grow * cand[slot].astype(F32) - drop * come[number, slot].astype(F32)
                ).astype(BF16)
                return 0

            lax.fori_loop(0, 2 * n_sec, cand_body, 0, unroll=2)

        def finish(wave):
            grow = coef[0, 0:1, :]
            drop = coef[1, 0:1, :]

            def body(local, _):
                wave[local] = (grow * own[step, local].astype(F32) - drop * image[local]).astype(BF16)
                return 0

            lax.fori_loop(0, held, body, 0, unroll=2)

        @pl.when(index == ITERS - 1)
        def _():
            finish(wave_one)
            energies[0:1, 0:1] = coef[2, 0:1, 0:1]
            hand = pltpu.make_async_remote_copy(
                src_ref=wave_one,
                dst_ref=prev_wave,
                send_sem=hand_sem.at[0],
                recv_sem=hand_sem.at[1],
                device_id=(following, me),
                device_id_type=MESH,
            )
            hand.start()

            def here(term, _):
                pltpu.make_async_copy(env.at[1, term], env.at[1, term], env_recv.at[term]).wait()
                return 0

            lax.fori_loop(0, terms, here, 0)
            hand.wait()

            @pl.when(sect != 0)
            def _():
                def transport(local, _):
                    wave = prev_wave[local]
                    turned = wave.astype(F32).T.astype(BF16)
                    for term in range(terms):
                        transit = jnp.dot(env[1, term, local], wave, preferred_element_type=F32)
                        passed = jnp.dot(turned, transit.astype(BF16), preferred_element_type=F32)
                        env[1, term, local] = (passed * (1.0 / BLK)).astype(BF16)
                    return 0

                lax.fori_loop(0, held, transport, 0)

            @pl.when(sect == 0)
            def _():
                def same(term, _):
                    env[1, term] = env[0, term]
                    return 0

                lax.fori_loop(0, terms, same, 0)

        @pl.when(index == 2 * ITERS - 1)
        def _():
            finish(wave_two)
            energies[0:1, 1:2] = coef[2, 0:1, 0:1]

        return 0

    lax.fori_loop(0, 2 * ITERS, iterate, 0)

    for number in (0, 1, 2, 3, 4, 5):
        left_here(number)

    def told(index, _):
        others = pl.ds(0, n_sec - 1)
        pltpu.make_async_copy(stat.at[index, others], stat.at[index, others], stat_send.at[index]).wait()
        return 0

    lax.fori_loop(0, 2 * ITERS, told, 0)

    def env_left(term, _):
        pltpu.make_async_copy(env.at[1, term], env.at[1, term], env_send.at[term]).wait()
        return 0

    lax.fori_loop(0, terms, env_left, 0)


def solution(mesh):
    n_sect, n_sec = mesh.shape["sect"], mesh.shape["sec"]
    wide = P("sect", "sec", None, None)
    deep = P("sect", None, "sec", None, None)

    def on_device(psi_first, psi_second, left_env, right_env, couplings, pair_sector):
        terms, held = left_env.shape[1], left_env.shape[2]
        block = (BLK, BLK)
        hbm = pl.BlockSpec(memory_space=pl.ANY)
        vmem = pl.BlockSpec(memory_space=pltpu.VMEM)
        smem = pl.BlockSpec(memory_space=pltpu.SMEM)
        dma = pltpu.SemaphoreType.DMA
        waves = jax.ShapeDtypeStruct((held,) + block, BF16)
        one, two, energy = pl.pallas_call(
            functools.partial(kernel, n_sect, n_sec),
            out_shape=(waves, waves, jax.ShapeDtypeStruct((1, 2), F32)),
            in_specs=[smem, smem, hbm, hbm, hbm, hbm],
            out_specs=(vmem, vmem, vmem),
            scratch_shapes=[
                pltpu.VMEM((2, terms, held) + block, BF16),
                pltpu.VMEM((terms, held) + block, BF16),
                pltpu.VMEM((2 * n_sec,) + block, BF16),
                pltpu.VMEM((6, 2 * n_sec) + block, BF16),
                pltpu.VMEM((2, held) + block, BF16),
                pltpu.VMEM((6, held) + block, BF16),
                pltpu.VMEM((held,) + block, F32),
                pltpu.VMEM((6, n_sec, 3, 8, BLK), F32),
                pltpu.VMEM((6, 3, 8, BLK), F32),
                pltpu.VMEM((3, 8, BLK), F32),
                pltpu.VMEM((held,) + block, BF16),
                dma((8,)),
                dma((6,)),
                dma((6,)),
                dma((6,)),
                dma((6,)),
                dma((terms,)),
                dma((terms,)),
                dma((2,)),
            ],
            compiler_params=pltpu.CompilerParams(
                collective_id=0, has_side_effects=True, vmem_limit_bytes=50 * 1024 * 1024
            ),
        )(
            couplings.reshape(-1),
            pair_sector.reshape(-1),
            psi_first[0],
            psi_second[0],
            left_env[0],
            right_env[0],
        )
        return (one[None], two[None], energy)

    return jax.shard_map(
        on_device,
        mesh=mesh,
        in_specs=(wide, wide, deep, deep, wide, P("sec", None)),
        out_specs=(wide, wide, P("sect", None)),
        check_vma=False,
    )
```

```python
import functools

import jax
import jax.numpy as jnp
from jax import lax
from jax.experimental import pallas as pl
from jax.experimental.pallas import tpu as pltpu
from jax.sharding import PartitionSpec as P

MESH = pl.DeviceIdType.MESH
BLK = 128
ITERS = 3
DESCENT = 0.1
F32 = jnp.float32
BF16 = jnp.bfloat16


def fold(tile):
    return jnp.sum(tile.reshape(tile.shape[0] // 8, 8, tile.shape[1]), axis=0)


def kernel(
    n_sect,
    n_sec,
    coup_in,
    pairs_in,
    psi_one,
    psi_two,
    left,
    right,
    wave_one,
    wave_two,
    energies,
    env,
    renv,
    cand,
    come,
    own,
    sent,
    image,
    stat,
    stat_own,
    coef,
    prev_wave,
    prev_turned,
    coup,
    pairs,
    load_sem,
    send_sem,
    recv_sem,
    relay_sem,
    stat_send,
    stat_recv,
    env_send,
    env_recv,
    hand_sem,
):
    sect = lax.axis_index("sect")
    me = lax.axis_index("sec")
    following = lax.rem(sect + 1, n_sect)
    previous = lax.rem(sect + n_sect - 1, n_sect)
    terms, held = left.shape[0], left.shape[1]
    total = float(n_sec * held * BLK * BLK)

    barrier = pltpu.get_barrier_semaphore()

    def greet(step, _):
        peer = lax.rem(me + step, n_sec)
        pl.semaphore_signal(barrier, inc=1, device_id=(sect, peer), device_id_type=MESH)
        return 0

    lax.fori_loop(1, n_sec, greet, 0)
    pl.semaphore_signal(barrier, inc=1, device_id=(following, me), device_id_type=MESH)
    pl.semaphore_signal(barrier, inc=1, device_id=(previous, me), device_id_type=MESH)

    def place(source, target, number):
        return pltpu.make_async_copy(source, target, load_sem.at[number])

    first = lax.rem(me, held)
    second = lax.rem(me + 1, held)
    loads = [
        place(psi_one, own.at[0], 0),
        place(psi_one.at[first], come.at[0, 2 * me], 1),
        place(psi_one.at[second], come.at[0, 2 * me + 1], 2),
        place(coup_in, coup, 8),
        place(pairs_in, pairs, 9),
        place(left, env.at[0], 3),
        place(right, renv, 4),
        place(psi_two, own.at[1], 5),
        place(psi_two.at[first], come.at[3, 2 * me], 6),
        place(psi_two.at[second], come.at[3, 2 * me + 1], 7),
    ]
    for load in loads:
        load.start()
    pl.semaphore_wait(barrier, n_sec + 1)

    def send_block(source, number, owner, kind, peer, done):
        pltpu.make_async_remote_copy(
            src_ref=source,
            dst_ref=come.at[number, 2 * owner + kind],
            send_sem=send_sem.at[number],
            recv_sem=done,
            device_id=(sect, peer),
            device_id_type=MESH,
        ).start()

    def send_sector(source, number, step):
        @pl.when(step != 1)
        def _():
            ahead = lax.rem(step + held - 1, held)
            send_block(source, number, me, 1, lax.rem(me + ahead, n_sec), relay_sem.at[number, ahead - 1])

        @pl.when(step != 0)
        def _():
            behind = held - step
            send_block(
                source, number, me, 0, lax.rem(me + n_sec - behind, n_sec), relay_sem.at[number, held - 2 + behind]
            )

        @pl.when(step == 0)
        def _():
            send_block(source, number, me, 1, lax.rem(me + n_sec - 1, n_sec), recv_sem.at[number])

        @pl.when(step == 1)
        def _():
            send_block(source, number, me, 0, lax.rem(me + 1, n_sec), recv_sem.at[number])

    def relay(number):
        def landed(lane):
            pltpu.make_async_copy(come.at[number, 0], come.at[number, 0], relay_sem.at[number, lane]).wait()

        def body(step, _):
            @pl.when(step != 1)
            def _():
                ahead = lax.rem(step + held - 1, held)
                owner = lax.rem(me + n_sec - ahead, n_sec)
                landed(ahead - 1)
                send_block(
                    come.at[number, 2 * owner + 1], number, owner, 0, lax.rem(me + 1, n_sec), recv_sem.at[number]
                )

            @pl.when(step != 0)
            def _():
                behind = held - step
                owner = lax.rem(me + behind, n_sec)
                landed(held - 2 + behind)
                send_block(
                    come.at[number, 2 * owner], number, owner, 1, lax.rem(me + n_sec - 1, n_sec), recv_sem.at[number]
                )

            return 0

        lax.fori_loop(0, held, body, 0)

    def send_start(source, number):
        def body(step, _):
            send_sector(source.at[lax.rem(me + step, held)], number, step)
            return 0

        lax.fori_loop(0, held, body, 0)

    send_start(psi_one, 0)

    def send_env(term, _):
        pltpu.make_async_remote_copy(
            src_ref=left.at[term],
            dst_ref=env.at[1, term],
            send_sem=env_send.at[term],
            recv_sem=env_recv.at[term],
            device_id=(following, me),
            device_id_type=MESH,
        ).start()
        return 0

    lax.fori_loop(0, terms, send_env, 0)

    lanes = lax.broadcasted_iota(jnp.int32, (1, BLK), 1)
    blocks = pl.ds(0, 2 * n_sec - 2)
    relayed = pl.ds(0, 2 * held)

    def arrived(number):
        pltpu.make_async_copy(come.at[number, relayed], come.at[number, relayed], recv_sem.at[number]).wait()

    def left_here(number):
        pltpu.make_async_copy(come.at[number, blocks], come.at[number, blocks], send_sem.at[number]).wait()

    for load in loads:
        load.wait()
    relay(0)

    def begin(step):
        arrived(3 * step)

        def body(slot, _):
            cand[slot] = come[3 * step, slot]
            return 0

        lax.fori_loop(0, 2 * n_sec, body, 0, unroll=2)
        coef[2] = jnp.zeros((8, BLK), F32)

    def iterate(index, _):
        step = lax.div(index, ITERS)
        turn = lax.rem(index, ITERS)
        number = index + 1

        @pl.when(turn == 0)
        def _():
            begin(step)

        @pl.when(index == ITERS - 1)
        def _():
            send_start(psi_two, 3)

        shift = coef[2, 0:1, :]

        def sector(turned, sums):
            local = lax.rem(me + turned, held)
            slots = []
            for pair in range(4):
                name = pairs[local, pair]
                slots.append(2 * lax.div(name, held) + lax.rem(name + n_sec - me, held))
            total_image = jnp.zeros((BLK, BLK), F32)
            for term in range(terms):
                mixed = None
                for pair in range(4):
                    part = coup[local, pair, term] * cand[slots[pair]].astype(F32)
                    mixed = part if mixed is None else mixed + part
                inner = jnp.dot(env[step, term, local], mixed.astype(BF16), preferred_element_type=F32)
                total_image = total_image + jnp.dot(
                    inner.astype(BF16), renv[term, local], preferred_element_type=F32
                )
            mine = own[step, local].astype(F32)
            rest = total_image - shift * mine

            @pl.when(turn < ITERS - 1)
            def _():
                sent[index, local] = rest.astype(BF16)

                @pl.when(turned < 2)
                def _():
                    come[number, 2 * me + turned] = rest.astype(BF16)

                send_sector(sent.at[index, local], number, turned)

            @pl.when(turn == ITERS - 1)
            def _():
                image[local] = rest

            square, cross, rests = sums
            return (square + fold(mine * mine), cross + fold(mine * rest), rests + fold(rest * rest))

        zero = jnp.zeros((8, BLK), F32)
        square, cross, rests = lax.fori_loop(0, held, sector, (zero, zero, zero))
        row = None
        for kind, value in enumerate((square, cross, rests)):
            part = jnp.where(lanes == kind, jnp.sum(value, axis=(0, 1), keepdims=True), 0.0)
            row = part if row is None else row + part
        stat_own[index] = row
        stat[index, me] = row

        def tell(offset, _):
            pltpu.make_async_remote_copy(
                src_ref=stat_own.at[index],
                dst_ref=stat.at[index, me],
                send_sem=stat_send.at[index],
                recv_sem=stat_recv.at[index],
                device_id=(sect, lax.rem(me + offset, n_sec)),
                device_id_type=MESH,
            ).start()
            return 0

        lax.fori_loop(1, n_sec, tell, 0)

        @pl.when(turn < ITERS - 1)
        def _():
            relay(number)

        others = pl.ds(0, n_sec - 1)
        pltpu.make_async_copy(stat.at[index, others], stat.at[index, others], stat_recv.at[index]).wait()
        table = jnp.sum(stat[index], axis=0)
        square, cross, rests = [
            jnp.broadcast_to(jnp.sum(jnp.where(lanes == kind, table, 0.0), axis=1, keepdims=True), (8, BLK))
            for kind in range(3)
        ]
        ratio = cross / square
        keep = 1.0 + DESCENT * ratio
        size = keep * keep * square - (2.0 * DESCENT) * keep * cross + (DESCENT * DESCENT) * rests
        scale = lax.rsqrt(size / total)
        coef[0] = keep * scale
        coef[1] = DESCENT * scale
        quot = coef[2] + ratio
        coef[2] = quot

        @pl.when(turn < ITERS - 1)
        def _():
            grow = coef[0, 0:1, :]
            drop = coef[1, 0:1, :]

            def own_body(local, _):
                own[step, local] = (
                    grow * own[step, local].astype(F32) - drop * sent[index, local].astype(F32)
                ).astype(BF16)
                return 0

            lax.fori_loop(0, held, own_body, 0, unroll=2)
            arrived(number)

            def cand_body(slot, _):
                cand[slot] = (
                    grow * cand[slot].astype(F32) - drop * come[number, slot].astype(F32)
                ).astype(BF16)
                return 0

            lax.fori_loop(0, 2 * n_sec, cand_body, 0, unroll=2)

        def finish(wave):
            grow = coef[0, 0:1, :]
            drop = coef[1, 0:1, :]

            def body(local, _):
                wave[local] = (grow * own[step, local].astype(F32) - drop * image[local]).astype(BF16)
                return 0

            lax.fori_loop(0, held, body, 0, unroll=2)

        @pl.when(index == ITERS - 1)
        def _():
            finish(wave_one)
            energies[0:1, 0:1] = coef[2, 0:1, 0:1]
            hand = pltpu.make_async_remote_copy(
                src_ref=wave_one,
                dst_ref=prev_wave,
                send_sem=hand_sem.at[0],
                recv_sem=hand_sem.at[1],
                device_id=(following, me),
                device_id_type=MESH,
            )
            hand.start()

            relay(3)
            hand.wait()

            def turn_wave(local, _):
                prev_turned[local] = prev_wave[local].astype(F32).T.astype(BF16)
                return 0

            lax.fori_loop(0, held, turn_wave, 0)

            def transport(term, _):
                pltpu.make_async_copy(env.at[1, term], env.at[1, term], env_recv.at[term]).wait()

                @pl.when(sect != 0)
                def _():
                    for local in range(held):
                        transit = jnp.dot(env[1, term, local], prev_wave[local], preferred_element_type=F32)
                        passed = jnp.dot(prev_turned[local], transit.astype(BF16), preferred_element_type=F32)
                        env[1, term, local] = (passed * (1.0 / BLK)).astype(BF16)

                @pl.when(sect == 0)
                def _():
                    env[1, term] = env[0, term]

                return 0

            lax.fori_loop(0, terms, transport, 0)

        @pl.when(index == 2 * ITERS - 1)
        def _():
            finish(wave_two)
            energies[0:1, 1:2] = coef[2, 0:1, 0:1]

        return 0

    lax.fori_loop(0, 2 * ITERS, iterate, 0)

    for number in (0, 1, 2, 3, 4, 5):
        left_here(number)

    def told(index, _):
        others = pl.ds(0, n_sec - 1)
        pltpu.make_async_copy(stat.at[index, others], stat.at[index, others], stat_send.at[index]).wait()
        return 0

    lax.fori_loop(0, 2 * ITERS, told, 0)

    def env_left(term, _):
        pltpu.make_async_copy(env.at[1, term], env.at[1, term], env_send.at[term]).wait()
        return 0

    lax.fori_loop(0, terms, env_left, 0)


def solution(mesh):
    n_sect, n_sec = mesh.shape["sect"], mesh.shape["sec"]
    wide = P("sect", "sec", None, None)
    deep = P("sect", None, "sec", None, None)

    def on_device(psi_first, psi_second, left_env, right_env, couplings, pair_sector):
        terms, held = left_env.shape[1], left_env.shape[2]
        block = (BLK, BLK)
        hbm = pl.BlockSpec(memory_space=pl.ANY)
        vmem = pl.BlockSpec(memory_space=pltpu.VMEM)
        dma = pltpu.SemaphoreType.DMA
        waves = jax.ShapeDtypeStruct((held,) + block, BF16)
        one, two, energy = pl.pallas_call(
            functools.partial(kernel, n_sect, n_sec),
            out_shape=(waves, waves, jax.ShapeDtypeStruct((1, 2), F32)),
            in_specs=[hbm] * 6,
            out_specs=(vmem, vmem, vmem),
            scratch_shapes=[
                pltpu.VMEM((2, terms, held) + block, BF16),
                pltpu.VMEM((terms, held) + block, BF16),
                pltpu.VMEM((2 * n_sec,) + block, BF16),
                pltpu.VMEM((6, 2 * n_sec) + block, BF16),
                pltpu.VMEM((2, held) + block, BF16),
                pltpu.VMEM((6, held) + block, BF16),
                pltpu.VMEM((held,) + block, F32),
                pltpu.VMEM((6, n_sec, 1, BLK), F32),
                pltpu.VMEM((6, 1, BLK), F32),
                pltpu.VMEM((3, 8, BLK), F32),
                pltpu.VMEM((held,) + block, BF16),
                pltpu.VMEM((held,) + block, BF16),
                pltpu.SMEM(couplings.shape[1:], F32),
                pltpu.SMEM(pair_sector.shape, jnp.int32),
                dma((10,)),
                dma((6,)),
                dma((6,)),
                dma((6, 2 * held - 2)),
                dma((6,)),
                dma((6,)),
                dma((terms,)),
                dma((terms,)),
                dma((2,)),
            ],
            compiler_params=pltpu.CompilerParams(
                collective_id=0, has_side_effects=True, vmem_limit_bytes=50 * 1024 * 1024
            ),
        )(
            couplings[0],
            pair_sector,
            psi_first[0],
            psi_second[0],
            left_env[0],
            right_env[0],
        )
        return (one[None], two[None], energy)

    return jax.shard_map(
        on_device,
        mesh=mesh,
        in_specs=(wide, wide, deep, deep, wide, P("sec", None)),
        out_specs=(wide, wide, P("sect", None)),
        check_vma=False,
    )
```

```python
import functools

import jax
import jax.numpy as jnp
from jax import lax
from jax.experimental import pallas as pl
from jax.experimental.pallas import tpu as pltpu
from jax.sharding import PartitionSpec as P

MESH = pl.DeviceIdType.MESH
BLK = 128
ITERS = 3
DESCENT = 0.1
F32 = jnp.float32
BF16 = jnp.bfloat16


def fold(tile):
    return jnp.sum(tile.reshape(tile.shape[0] // 8, 8, tile.shape[1]), axis=0)


def kernel(
    side,
    n_sect,
    n_sec,
    coup_in,
    pairs_in,
    psi_one,
    psi_two,
    left,
    right,
    wave_one,
    wave_two,
    energies,
    env,
    renv,
    cand,
    come,
    own,
    sent,
    image,
    stat,
    stat_own,
    coef,
    prev_wave,
    hop_one,
    hop_two,
    coup,
    pairs,
    load_sem,
    send_sem,
    recv_sem,
    relay_sem,
    stat_send,
    stat_recv,
    env_send,
    env_recv,
    hop_send,
    hop_recv,
    hand_send,
    hand_recv,
):
    sect = lax.axis_index("sect")
    me = lax.axis_index("sec")
    following = lax.rem(sect + 1, n_sect)
    previous = lax.rem(sect + n_sect - 1, n_sect)
    terms, held = left.shape[0], left.shape[1]
    round_terms = hop_one.shape[0]
    near_terms = terms - round_terms
    batches = env_send.shape[0]
    column, row_at = lax.rem(sect, side), lax.div(sect, side)
    below = row_at * side + lax.rem(column + side - 1, side)
    above = row_at * side + lax.rem(column + 1, side)
    turns = lax.div(lax.rem(column + side - 2, side), side - 1)
    turned_from = lax.div(lax.rem(column + side - 1, side), side - 1)
    hop_to = turns * lax.rem(row_at + 1, side) * side + (1 - turns) * below
    hop_from = turned_from * (lax.rem(row_at + side - 1, side) * side + 1) + (1 - turned_from) * above
    half = n_sec // 2
    total = float(n_sec * held * BLK * BLK)

    barrier = pltpu.get_barrier_semaphore()

    def greet(step, _):
        peer = lax.rem(me + step, n_sec)
        pl.semaphore_signal(barrier, inc=1, device_id=(sect, peer), device_id_type=MESH)
        return 0

    lax.fori_loop(1, n_sec, greet, 0)
    for section in (following, previous, below, above, hop_to, hop_from):
        pl.semaphore_signal(barrier, inc=1, device_id=(section, me), device_id_type=MESH)

    def place(source, target, number):
        return pltpu.make_async_copy(source, target, load_sem.at[number])

    first = lax.rem(me, held)
    second = lax.rem(me + 1, held)
    loads = [
        place(psi_one, own.at[0], 0),
        place(psi_one.at[first], come.at[0, 2 * me], 1),
        place(psi_one.at[second], come.at[0, 2 * me + 1], 2),
        place(coup_in, coup, 8),
        place(pairs_in, pairs, 9),
        place(left, env.at[0], 3),
        place(right, renv, 4),
        place(psi_two, own.at[1], 5),
        place(psi_two.at[first], come.at[3, 2 * me], 6),
        place(psi_two.at[second], come.at[3, 2 * me + 1], 7),
    ]
    for load in loads:
        load.start()
    pl.semaphore_wait(barrier, n_sec + 5)

    def send_block(source, number, owner, kind, peer, done):
        pltpu.make_async_remote_copy(
            src_ref=source,
            dst_ref=come.at[number, 2 * owner + kind],
            send_sem=send_sem.at[number],
            recv_sem=done,
            device_id=(sect, peer),
            device_id_type=MESH,
        ).start()

    def send_sector(source, number, step):
        @pl.when(step != 1)
        def _():
            ahead = lax.rem(step + held - 1, held)
            send_block(source, number, me, 1, lax.rem(me + ahead, n_sec), relay_sem.at[number, ahead - 1])

        @pl.when(step != 0)
        def _():
            behind = held - step
            send_block(
                source, number, me, 0, lax.rem(me + n_sec - behind, n_sec), relay_sem.at[number, held - 2 + behind]
            )

        @pl.when(step == 0)
        def _():
            send_block(source, number, me, 1, lax.rem(me + n_sec - 1, n_sec), recv_sem.at[number])

        @pl.when(step == 1)
        def _():
            send_block(source, number, me, 0, lax.rem(me + 1, n_sec), recv_sem.at[number])

    def relay(number, between=None):
        def landed(lane):
            pltpu.make_async_copy(come.at[number, 0], come.at[number, 0], relay_sem.at[number, lane]).wait()

        def body(step, _):
            @pl.when(step != 1)
            def _():
                ahead = lax.rem(step + held - 1, held)
                owner = lax.rem(me + n_sec - ahead, n_sec)
                landed(ahead - 1)
                send_block(
                    come.at[number, 2 * owner + 1], number, owner, 0, lax.rem(me + 1, n_sec), recv_sem.at[number]
                )

            @pl.when(step != 0)
            def _():
                behind = held - step
                owner = lax.rem(me + behind, n_sec)
                landed(held - 2 + behind)
                send_block(
                    come.at[number, 2 * owner], number, owner, 1, lax.rem(me + n_sec - 1, n_sec), recv_sem.at[number]
                )

            if between is not None:
                pl.when(step == 1)(between)
            return 0

        lax.fori_loop(0, held, body, 0)

    def send_start(source, number):
        def body(step, _):
            send_sector(source.at[lax.rem(me + step, held)], number, step)
            return 0

        lax.fori_loop(0, held, body, 0)

    send_start(psi_one, 0)

    def batch(number):
        low = number * near_terms // batches
        span = pl.ds(low, (number + 1) * near_terms // batches - low)
        return pltpu.make_async_remote_copy(
            src_ref=left.at[span],
            dst_ref=env.at[1, span],
            send_sem=env_send.at[number],
            recv_sem=env_recv.at[number],
            device_id=(following, me),
            device_id_type=MESH,
        )

    batch(0).start()
    tail = pl.ds(near_terms, round_terms)

    def hop(number, section):
        source = (left.at[tail], hop_one, hop_two)[number]
        target = (hop_one, hop_two, env.at[1, tail])[number]
        return pltpu.make_async_remote_copy(
            src_ref=source,
            dst_ref=target,
            send_sem=hop_send.at[number],
            recv_sem=hop_recv.at[number],
            device_id=(section, me),
            device_id_type=MESH,
        )

    hop(0, below).start()

    lanes = lax.broadcasted_iota(jnp.int32, (1, BLK), 1)
    blocks = pl.ds(0, 2 * n_sec - 2)
    relayed = pl.ds(0, 2 * held)

    def arrived(number):
        pltpu.make_async_copy(come.at[number, relayed], come.at[number, relayed], recv_sem.at[number]).wait()

    def left_here(number):
        pltpu.make_async_copy(come.at[number, blocks], come.at[number, blocks], send_sem.at[number]).wait()

    for load in loads:
        load.wait()
    relay(0)
    batch(1).start()

    def begin(step):
        arrived(3 * step)

        def body(slot, _):
            cand[slot] = come[3 * step, slot]
            return 0

        lax.fori_loop(0, 2 * n_sec, body, 0, unroll=2)
        coef[2] = jnp.zeros((8, BLK), F32)

    def hand(local):
        return pltpu.make_async_remote_copy(
            src_ref=wave_one.at[local],
            dst_ref=prev_wave.at[local],
            send_sem=hand_send,
            recv_sem=hand_recv.at[local],
            device_id=(following, me),
            device_id_type=MESH,
        )

    def iterate(index, _):
        step = lax.div(index, ITERS)
        turn = lax.rem(index, ITERS)
        number = index + 1

        @pl.when(turn == 0)
        def _():
            begin(step)

        shift = coef[2, 0:1, :]

        @pl.when(index == ITERS)
        def _():
            for number in range(batches):
                batch(number).wait_recv()
            hop(2, hop_to).wait_recv()

        def sector(turned, sums):
            local = lax.rem(me + turned, held)

            @pl.when(index == ITERS)
            def _():
                hand(local).wait_recv()

                @pl.when(sect != 0)
                def _():
                    wave = prev_wave[local]
                    flipped = wave.astype(F32).T.astype(BF16)
                    for term in range(terms):
                        transit = jnp.dot(env[1, term, local], wave, preferred_element_type=F32)
                        passed = jnp.dot(flipped, transit.astype(BF16), preferred_element_type=F32)
                        env[1, term, local] = (passed * (1.0 / BLK)).astype(BF16)

                @pl.when(sect == 0)
                def _():
                    for term in range(terms):
                        env[1, term, local] = env[0, term, local]

            slots = []
            for pair in range(4):
                name = pairs[pair, local]
                slots.append(2 * lax.div(name, held) + lax.rem(name + n_sec - me, held))
            total_image = jnp.zeros((BLK, BLK), F32)
            for term in range(terms):
                mixed = None
                for pair in range(4):
                    part = coup[local, pair, term] * cand[slots[pair]].astype(F32)
                    mixed = part if mixed is None else mixed + part
                inner = jnp.dot(env[step, term, local], mixed.astype(BF16), preferred_element_type=F32)
                total_image = total_image + jnp.dot(
                    inner.astype(BF16), renv[term, local], preferred_element_type=F32
                )
            mine = own[step, local].astype(F32)
            rest = total_image - shift * mine

            @pl.when(turn < ITERS - 1)
            def _():
                sent[index, local] = rest.astype(BF16)

                @pl.when(turned < 2)
                def _():
                    come[number, 2 * me + turned] = rest.astype(BF16)

                send_sector(sent.at[index, local], number, turned)

            @pl.when(turn == ITERS - 1)
            def _():
                image[local] = rest

            square, cross, rests = sums
            return (square + fold(mine * mine), cross + fold(mine * rest), rests + fold(rest * rest))

        zero = jnp.zeros((8, BLK), F32)
        square, cross, rests = lax.fori_loop(0, held, sector, (zero, zero, zero))
        row = None
        for kind, value in enumerate((square, cross, rests)):
            part = jnp.where(lanes == kind, jnp.sum(value, axis=(0, 1), keepdims=True), 0.0)
            row = part if row is None else row + part
        stat_own[index] = row
        stat[index, me] = row

        def tell(order, _):
            offset = half + (1 - 2 * lax.rem(order, 2)) * lax.div(order + 1, 2)
            pltpu.make_async_remote_copy(
                src_ref=stat_own.at[index],
                dst_ref=stat.at[index, me],
                send_sem=stat_send.at[index],
                recv_sem=stat_recv.at[index],
                device_id=(sect, lax.rem(me + offset, n_sec)),
                device_id_type=MESH,
            ).start()
            return 0

        lax.fori_loop(0, n_sec - 1, tell, 0)

        @pl.when(index == 0)
        def _():
            def pass_on():
                hop(0, below).wait_recv()
                hop(1, below).start()

            relay(number, pass_on)
            batch(2).start()

        @pl.when(index == 1)
        def _():
            def pass_on():
                hop(1, below).wait_recv()
                hop(2, hop_to).start()

            relay(number, pass_on)
            batch(3).start()
            send_start(psi_two, 3)

        @pl.when(index >= ITERS)
        def _():
            @pl.when(turn < ITERS - 1)
            def _():
                relay(number)

        others = pl.ds(0, n_sec - 1)
        pltpu.make_async_copy(stat.at[index, others], stat.at[index, others], stat_recv.at[index]).wait()
        table = jnp.sum(stat[index], axis=0)
        square, cross, rests = [
            jnp.broadcast_to(jnp.sum(jnp.where(lanes == kind, table, 0.0), axis=1, keepdims=True), (8, BLK))
            for kind in range(3)
        ]
        ratio = cross / square
        keep = 1.0 + DESCENT * ratio
        size = keep * keep * square - (2.0 * DESCENT) * keep * cross + (DESCENT * DESCENT) * rests
        scale = lax.rsqrt(size / total)
        coef[0] = keep * scale
        coef[1] = DESCENT * scale
        quot = coef[2] + ratio
        coef[2] = quot

        @pl.when(turn < ITERS - 1)
        def _():
            grow = coef[0, 0:1, :]
            drop = coef[1, 0:1, :]

            def own_body(local, _):
                own[step, local] = (
                    grow * own[step, local].astype(F32) - drop * sent[index, local].astype(F32)
                ).astype(BF16)
                return 0

            lax.fori_loop(0, held, own_body, 0, unroll=2)
            arrived(number)

            def cand_body(slot, _):
                cand[slot] = (
                    grow * cand[slot].astype(F32) - drop * come[number, slot].astype(F32)
                ).astype(BF16)
                return 0

            lax.fori_loop(0, 2 * n_sec, cand_body, 0, unroll=2)

        def finish(wave, onward):
            grow = coef[0, 0:1, :]
            drop = coef[1, 0:1, :]

            def body(turned, _):
                local = lax.rem(me + turned, held)
                wave[local] = (grow * own[step, local].astype(F32) - drop * image[local]).astype(BF16)
                if onward:
                    hand(local).start()
                return 0

            lax.fori_loop(0, held, body, 0)

        @pl.when(index == ITERS - 1)
        def _():
            finish(wave_one, True)
            energies[0:1, 0:1] = coef[2, 0:1, 0:1]
            relay(3)

        @pl.when(index == 2 * ITERS - 1)
        def _():
            finish(wave_two, False)
            energies[0:1, 1:2] = coef[2, 0:1, 0:1]

        return 0

    lax.fori_loop(0, 2 * ITERS, iterate, 0)

    for number in (0, 1, 2, 3, 4, 5):
        left_here(number)

    def told(index, _):
        others = pl.ds(0, n_sec - 1)
        pltpu.make_async_copy(stat.at[index, others], stat.at[index, others], stat_send.at[index]).wait()
        return 0

    lax.fori_loop(0, 2 * ITERS, told, 0)

    for number in range(batches):
        batch(number).wait_send()
    for number, section in ((0, below), (1, below), (2, hop_to)):
        hop(number, section).wait_send()
    pltpu.make_async_copy(prev_wave, prev_wave, hand_send).wait()


def solution(mesh):
    n_sect, n_sec = mesh.shape["sect"], mesh.shape["sec"]
    side = int(round(n_sect**0.5))
    wide = P("sect", "sec", None, None)
    deep = P("sect", None, "sec", None, None)

    def on_device(psi_first, psi_second, left_env, right_env, couplings, pair_sector):
        terms, held = left_env.shape[1], left_env.shape[2]
        block = (BLK, BLK)
        hbm = pl.BlockSpec(memory_space=pltpu.HBM)
        round_terms = terms * 3 // 14
        vmem = pl.BlockSpec(memory_space=pltpu.VMEM)
        dma = pltpu.SemaphoreType.DMA
        waves = jax.ShapeDtypeStruct((held,) + block, BF16)
        one, two, energy = pl.pallas_call(
            functools.partial(kernel, side, n_sect, n_sec),
            out_shape=(waves, waves, jax.ShapeDtypeStruct((1, 2), F32)),
            in_specs=[hbm] * 6,
            out_specs=(vmem, vmem, vmem),
            scratch_shapes=[
                pltpu.VMEM((2, terms, held) + block, BF16),
                pltpu.VMEM((terms, held) + block, BF16),
                pltpu.VMEM((2 * n_sec,) + block, BF16),
                pltpu.VMEM((6, 2 * n_sec) + block, BF16),
                pltpu.VMEM((2, held) + block, BF16),
                pltpu.VMEM((6, held) + block, BF16),
                pltpu.VMEM((held,) + block, F32),
                pltpu.VMEM((6, n_sec, 1, BLK), F32),
                pltpu.VMEM((6, 1, BLK), F32),
                pltpu.VMEM((3, 8, BLK), F32),
                pltpu.VMEM((held,) + block, BF16),
                pltpu.VMEM((round_terms, held) + block, BF16),
                pltpu.VMEM((round_terms, held) + block, BF16),
                pltpu.SMEM(couplings.shape[1:], F32),
                pltpu.SMEM(pair_sector.shape[::-1], jnp.int32),
                dma((10,)),
                dma((6,)),
                dma((6,)),
                dma((6, 2 * held - 2)),
                dma((6,)),
                dma((6,)),
                dma((4,)),
                dma((4,)),
                dma((3,)),
                dma((3,)),
                dma,
                dma((held,)),
            ],
            compiler_params=pltpu.CompilerParams(
                collective_id=0, has_side_effects=True, vmem_limit_bytes=60 * 1024 * 1024
            ),
        )(
            couplings[0],
            pair_sector.T,
            psi_first[0],
            psi_second[0],
            left_env[0],
            right_env[0],
        )
        return (one[None], two[None], energy)

    return jax.shard_map(
        on_device,
        mesh=mesh,
        in_specs=(wide, wide, deep, deep, wide, P("sec", None)),
        out_specs=(wide, wide, P("sect", None)),
        check_vma=False,
    )
```

```python
import functools

import jax
import jax.numpy as jnp
from jax import lax
from jax.experimental import pallas as pl
from jax.experimental.pallas import tpu as pltpu
from jax.sharding import PartitionSpec as P

MESH = pl.DeviceIdType.MESH
BLK = 128
ITERS = 3
DESCENT = 0.1
F32 = jnp.float32
BF16 = jnp.bfloat16


def fold(tile):
    return jnp.sum(tile.reshape(tile.shape[0] // 8, 8, tile.shape[1]), axis=0)


def kernel(
    side,
    n_sect,
    n_sec,
    coup_in,
    pairs_in,
    psi_one,
    psi_two,
    left,
    right,
    wave_one,
    wave_two,
    energies,
    env,
    renv,
    cand,
    come,
    own,
    sent,
    image,
    stat,
    stat_own,
    coef,
    parts,
    prev_wave,
    hop_one,
    hop_two,
    coup,
    pairs,
    load_sem,
    send_sem,
    recv_sem,
    relay_sem,
    stat_send,
    stat_recv,
    env_send,
    env_recv,
    hop_send,
    hop_recv,
    hand_send,
    hand_recv,
):
    sect = lax.axis_index("sect")
    me = lax.axis_index("sec")
    following = lax.rem(sect + 1, n_sect)
    previous = lax.rem(sect + n_sect - 1, n_sect)
    terms, held = left.shape[0], left.shape[1]
    near_terms = terms - hop_one.shape[0]
    column, row_at = lax.rem(sect, side), lax.div(sect, side)
    below = row_at * side + lax.rem(column + side - 1, side)
    above = row_at * side + lax.rem(column + 1, side)
    turns = lax.div(lax.rem(column + side - 2, side), side - 1)
    turned_from = lax.div(lax.rem(column + side - 1, side), side - 1)
    hop_to = turns * lax.rem(row_at + 1, side) * side + (1 - turns) * below
    hop_from = turned_from * (lax.rem(row_at + side - 1, side) * side + 1) + (1 - turned_from) * above
    half = n_sec // 2
    total = float(n_sec * held * BLK * BLK)

    def far_first(order):
        return lax.rem(held + (1 - 2 * lax.rem(order, 2)) * lax.div(order + 1, 2), held)

    barrier = pltpu.get_barrier_semaphore()

    def greet(step, _):
        peer = lax.rem(me + step, n_sec)
        pl.semaphore_signal(barrier, inc=1, device_id=(sect, peer), device_id_type=MESH)
        return 0

    lax.fori_loop(1, n_sec, greet, 0)
    for section in (following, previous, below, above, hop_to, hop_from):
        pl.semaphore_signal(barrier, inc=1, device_id=(section, me), device_id_type=MESH)

    def place(source, target, number):
        return pltpu.make_async_copy(source, target, load_sem.at[number])

    first = lax.rem(me, held)
    second = lax.rem(me + 1, held)
    loads = [
        place(psi_one, own.at[0], 0),
        place(psi_one.at[first], come.at[0, 2 * me], 1),
        place(psi_one.at[second], come.at[0, 2 * me + 1], 2),
        place(coup_in, coup, 8),
        place(pairs_in, pairs, 9),
        place(left, env.at[0], 3),
        place(right, renv, 4),
        place(psi_two, own.at[1], 5),
        place(psi_two.at[first], come.at[3, 2 * me], 6),
        place(psi_two.at[second], come.at[3, 2 * me + 1], 7),
    ]
    for load in loads:
        load.start()
    pl.semaphore_wait(barrier, n_sec + 5)

    def send_block(source, number, owner, kind, peer, done):
        pltpu.make_async_remote_copy(
            src_ref=source,
            dst_ref=come.at[number, 2 * owner + kind],
            send_sem=send_sem.at[number],
            recv_sem=done,
            device_id=(sect, peer),
            device_id_type=MESH,
        ).start()

    def send_sector(source, number, step):
        @pl.when(step != 1)
        def _():
            ahead = lax.rem(step + held - 1, held)
            send_block(source, number, me, 1, lax.rem(me + ahead, n_sec), relay_sem.at[number, ahead - 1])

        @pl.when(step != 0)
        def _():
            behind = held - step
            send_block(
                source, number, me, 0, lax.rem(me + n_sec - behind, n_sec), relay_sem.at[number, held - 2 + behind]
            )

        @pl.when(step == 0)
        def _():
            send_block(source, number, me, 1, lax.rem(me + n_sec - 1, n_sec), recv_sem.at[number])

        @pl.when(step == 1)
        def _():
            send_block(source, number, me, 0, lax.rem(me + 1, n_sec), recv_sem.at[number])

    def relay(number, between=None):
        def landed(lane):
            pltpu.make_async_copy(come.at[number, 0], come.at[number, 0], relay_sem.at[number, lane]).wait()

        def body(order, _):
            step = far_first(order)

            @pl.when(step != 1)
            def _():
                ahead = lax.rem(step + held - 1, held)
                owner = lax.rem(me + n_sec - ahead, n_sec)
                landed(ahead - 1)
                send_block(
                    come.at[number, 2 * owner + 1], number, owner, 0, lax.rem(me + 1, n_sec), recv_sem.at[number]
                )

            @pl.when(step != 0)
            def _():
                behind = held - step
                owner = lax.rem(me + behind, n_sec)
                landed(held - 2 + behind)
                send_block(
                    come.at[number, 2 * owner], number, owner, 1, lax.rem(me + n_sec - 1, n_sec), recv_sem.at[number]
                )

            if between is not None:
                pl.when(order == 1)(between)
            return 0

        lax.fori_loop(0, held, body, 0)

    def send_start(source, number, low, high):
        def body(order, _):
            step = far_first(order)
            send_sector(source.at[lax.rem(me + step, held)], number, step)
            return 0

        lax.fori_loop(low, high, body, 0)

    send_start(psi_one, 0, 0, held)

    def position(order):
        return lax.rem(me + far_first(order), held)

    near = pl.ds(0, near_terms)
    tail = pl.ds(near_terms, terms - near_terms)

    def near_env(order):
        return pltpu.make_async_remote_copy(
            src_ref=left.at[near, position(order)],
            dst_ref=env.at[1, near, position(order)],
            send_sem=env_send.at[order],
            recv_sem=env_recv.at[order],
            device_id=(following, me),
            device_id_type=MESH,
        )

    def hop(number):
        return pltpu.make_async_remote_copy(
            src_ref=(left.at[tail], hop_one, hop_two)[number],
            dst_ref=(hop_one, hop_two, env.at[1, tail])[number],
            send_sem=hop_send.at[number],
            recv_sem=hop_recv.at[number],
            device_id=(hop_to if number == 2 else below, me),
            device_id_type=MESH,
        )

    def pass_on(number):
        hop(number).wait_recv()
        hop(number + 1).start()

    hop(0).start()
    near_env(0).start()
    near_env(1).start()
    lanes = lax.broadcasted_iota(jnp.int32, (1, BLK), 1)
    blocks = pl.ds(0, 2 * n_sec - 2)
    relayed = pl.ds(0, 2 * held)

    def arrived(number):
        pltpu.make_async_copy(come.at[number, relayed], come.at[number, relayed], recv_sem.at[number]).wait()

    def left_here(number):
        pltpu.make_async_copy(come.at[number, blocks], come.at[number, blocks], send_sem.at[number]).wait()

    for load in loads:
        load.wait()
    relay(0)
    near_env(2).start()
    near_env(3).start()

    def begin(step):
        arrived(3 * step)

        def body(slot, _):
            cand[slot] = come[3 * step, slot]
            return 0

        lax.fori_loop(0, 2 * n_sec, body, 0, unroll=2)
        coef[2] = jnp.zeros((8, BLK), F32)

    def hand(local):
        return pltpu.make_async_remote_copy(
            src_ref=wave_one.at[local],
            dst_ref=prev_wave.at[local],
            send_sem=hand_send,
            recv_sem=hand_recv.at[local],
            device_id=(following, me),
            device_id_type=MESH,
        )

    def iterate(index, _):
        step = lax.div(index, ITERS)
        turn = lax.rem(index, ITERS)
        number = index + 1

        @pl.when(turn == 0)
        def _():
            begin(step)

        shift = coef[2, 0:1, :]

        def products(local):
            slots = []
            for pair in range(4):
                name = pairs[pair, local]
                slots.append(2 * lax.div(name, held) + lax.rem(name + n_sec - me, held))
            total_image = jnp.zeros((BLK, BLK), F32)
            for term in range(terms):
                mixed = None
                for pair in range(4):
                    part = coup[local, pair, term] * cand[slots[pair]].astype(F32)
                    mixed = part if mixed is None else mixed + part
                inner = jnp.dot(env[step, term, local], mixed.astype(BF16), preferred_element_type=F32)
                total_image = total_image + jnp.dot(
                    inner.astype(BF16), renv[term, local], preferred_element_type=F32
                )
            return total_image

        def sector(order, sums):
            turned = far_first(order)
            local = lax.rem(me + turned, held)

            @pl.when(index == ITERS)
            def _():
                hand(local).wait_recv()

                near_env(order).wait_recv()

                @pl.when(order == 0)
                def _():
                    hop(2).wait_recv()

                @pl.when(sect != 0)
                def _():
                    wave = prev_wave[local]
                    flipped = wave.astype(F32).T.astype(BF16)
                    for term in range(terms):
                        transit = jnp.dot(env[1, term, local], wave, preferred_element_type=F32)
                        passed = jnp.dot(flipped, transit.astype(BF16), preferred_element_type=F32)
                        env[1, term, local] = (passed * (1.0 / BLK)).astype(BF16)

                @pl.when(sect == 0)
                def _():
                    for term in range(terms):
                        env[1, term, local] = env[0, term, local]

            total_image = products(local)
            mine = own[step, local].astype(F32)
            rest = total_image - shift * mine

            sent[index, local] = rest.astype(BF16)

            @pl.when(turned < 2)
            def _():
                come[number, 2 * me + turned] = rest.astype(BF16)

            send_sector(sent.at[index, local], number, turned)
            square, cross, rests = sums
            return (square + fold(mine * mine), cross + fold(mine * rest), rests + fold(rest * rest))

        def last_sector(local, sums):
            mine = own[step, local].astype(F32)
            rest = products(local) - shift * mine
            image[local] = rest
            square, cross, rests = sums
            return (square + fold(mine * mine), cross + fold(mine * rest), rests + fold(rest * rest))

        zero = jnp.zeros((8, BLK), F32)

        def total_up(body, unroll):
            for kind, value in enumerate(lax.fori_loop(0, held, body, (zero, zero, zero), unroll=unroll)):
                parts[kind] = value

        @pl.when(turn < ITERS - 1)
        def _():
            total_up(sector, 1)

        @pl.when(turn == ITERS - 1)
        def _():
            total_up(last_sector, 4)

        row = None
        for kind in range(3):
            part = jnp.where(lanes == kind, jnp.sum(parts[kind], axis=(0, 1), keepdims=True), 0.0)
            row = part if row is None else row + part
        stat_own[index] = row
        stat[index, me] = row

        def tell(order, _):
            offset = half + (1 - 2 * lax.rem(order, 2)) * lax.div(order + 1, 2)
            pltpu.make_async_remote_copy(
                src_ref=stat_own.at[index],
                dst_ref=stat.at[index, me],
                send_sem=stat_send.at[index],
                recv_sem=stat_recv.at[index],
                device_id=(sect, lax.rem(me + offset, n_sec)),
                device_id_type=MESH,
            ).start()
            return 0

        lax.fori_loop(0, n_sec - 1, tell, 0)

        @pl.when(index == 0)
        def _():
            relay(number, functools.partial(pass_on, 0))
            near_env(4).start()
            near_env(5).start()

        @pl.when(index == 1)
        def _():
            relay(number, functools.partial(pass_on, 1))
            near_env(6).start()
            near_env(7).start()
            send_start(psi_two, 3, 0, held)

        @pl.when(index >= ITERS)
        def _():
            @pl.when(turn < ITERS - 1)
            def _():
                relay(number)

        others = pl.ds(0, n_sec - 1)
        pltpu.make_async_copy(stat.at[index, others], stat.at[index, others], stat_recv.at[index]).wait()
        table = jnp.sum(stat[index], axis=0)
        square, cross, rests = [
            jnp.broadcast_to(jnp.sum(jnp.where(lanes == kind, table, 0.0), axis=1, keepdims=True), (8, BLK))
            for kind in range(3)
        ]
        ratio = cross / square
        keep = 1.0 + DESCENT * ratio
        size = keep * keep * square - (2.0 * DESCENT) * keep * cross + (DESCENT * DESCENT) * rests
        scale = lax.rsqrt(size / total)
        coef[0] = keep * scale
        coef[1] = DESCENT * scale
        quot = coef[2] + ratio
        coef[2] = quot

        @pl.when(turn < ITERS - 1)
        def _():
            grow = coef[0, 0:1, :]
            drop = coef[1, 0:1, :]

            def own_body(local, _):
                own[step, local] = (
                    grow * own[step, local].astype(F32) - drop * sent[index, local].astype(F32)
                ).astype(BF16)
                return 0

            lax.fori_loop(0, held, own_body, 0, unroll=2)
            def renew(slot):
                cand[slot] = (
                    grow * cand[slot].astype(F32) - drop * come[number, slot].astype(F32)
                ).astype(BF16)

            renew(2 * me)
            renew(2 * me + 1)

            def direct(away, _):
                renew(2 * lax.rem(me + n_sec - away, n_sec) + 1)
                renew(2 * lax.rem(me + away, n_sec))
                return 0

            lax.fori_loop(1, held, direct, 0)
            arrived(number)

            def relayed_on(away, _):
                renew(2 * lax.rem(me + n_sec - away, n_sec))
                renew(2 * lax.rem(me + away, n_sec) + 1)
                return 0

            lax.fori_loop(1, held + 1, relayed_on, 0)

        def finish(wave, onward):
            grow = coef[0, 0:1, :]
            drop = coef[1, 0:1, :]

            def body(order, _):
                local = lax.rem(me + far_first(order), held)
                wave[local] = (grow * own[step, local].astype(F32) - drop * image[local]).astype(BF16)
                if onward:
                    hand(local).start()
                return 0

            lax.fori_loop(0, held, body, 0)

        @pl.when(index == ITERS - 1)
        def _():
            finish(wave_one, True)
            energies[0:1, 0:1] = coef[2, 0:1, 0:1]
            relay(3)

        @pl.when(index == 2 * ITERS - 1)
        def _():
            finish(wave_two, False)
            energies[0:1, 1:2] = coef[2, 0:1, 0:1]

        return 0

    lax.fori_loop(0, 2 * ITERS, iterate, 0)

    for number in (0, 1, 2, 3, 4, 5):
        left_here(number)

    def told(index, _):
        others = pl.ds(0, n_sec - 1)
        pltpu.make_async_copy(stat.at[index, others], stat.at[index, others], stat_send.at[index]).wait()
        return 0

    lax.fori_loop(0, 2 * ITERS, told, 0)

    for order in range(held):
        near_env(order).wait_send()
    for number in range(3):
        hop(number).wait_send()
    pltpu.make_async_copy(prev_wave, prev_wave, hand_send).wait()


def solution(mesh):
    n_sect, n_sec = mesh.shape["sect"], mesh.shape["sec"]
    side = int(round(n_sect**0.5))
    wide = P("sect", "sec", None, None)
    deep = P("sect", None, "sec", None, None)

    def on_device(psi_first, psi_second, left_env, right_env, couplings, pair_sector):
        terms, held = left_env.shape[1], left_env.shape[2]
        block = (BLK, BLK)
        hbm = pl.BlockSpec(memory_space=pltpu.HBM)
        far_terms = terms * 3 // 14
        vmem = pl.BlockSpec(memory_space=pltpu.VMEM)
        dma = pltpu.SemaphoreType.DMA
        waves = jax.ShapeDtypeStruct((held,) + block, BF16)
        one, two, energy = pl.pallas_call(
            functools.partial(kernel, side, n_sect, n_sec),
            out_shape=(waves, waves, jax.ShapeDtypeStruct((1, 2), F32)),
            in_specs=[hbm] * 6,
            out_specs=(vmem, vmem, vmem),
            scratch_shapes=[
                pltpu.VMEM((2, terms, held) + block, BF16),
                pltpu.VMEM((terms, held) + block, BF16),
                pltpu.VMEM((2 * n_sec,) + block, BF16),
                pltpu.VMEM((6, 2 * n_sec) + block, BF16),
                pltpu.VMEM((2, held) + block, BF16),
                pltpu.VMEM((6, held) + block, BF16),
                pltpu.VMEM((held,) + block, F32),
                pltpu.VMEM((6, n_sec, 1, BLK), F32),
                pltpu.VMEM((6, 1, BLK), F32),
                pltpu.VMEM((3, 8, BLK), F32),
                pltpu.VMEM((3, 8, BLK), F32),
                pltpu.VMEM((held,) + block, BF16),
                pltpu.VMEM((far_terms, held) + block, BF16),
                pltpu.VMEM((far_terms, held) + block, BF16),
                pltpu.SMEM(couplings.shape[1:], F32),
                pltpu.SMEM(pair_sector.shape[::-1], jnp.int32),
                dma((10,)),
                dma((6,)),
                dma((6,)),
                dma((6, 2 * held - 2)),
                dma((6,)),
                dma((6,)),
                dma((held,)),
                dma((held,)),
                dma((3,)),
                dma((3,)),
                dma,
                dma((held,)),
            ],
            compiler_params=pltpu.CompilerParams(
                collective_id=0, has_side_effects=True, vmem_limit_bytes=213 * 256 * 1024
            ),
        )(
            couplings[0],
            pair_sector.T,
            psi_first[0],
            psi_second[0],
            left_env[0],
            right_env[0],
        )
        return (one[None], two[None], energy)

    return jax.shard_map(
        on_device,
        mesh=mesh,
        in_specs=(wide, wide, deep, deep, wide, P("sec", None)),
        out_specs=(wide, wide, P("sect", None)),
        check_vma=False,
    )
```

```python
import functools

import jax
import jax.numpy as jnp
from jax import lax
from jax.experimental import pallas as pl
from jax.experimental.pallas import tpu as pltpu
from jax.sharding import PartitionSpec as P

MESH = pl.DeviceIdType.MESH
BLK = 128
ITERS = 3
DESCENT = 0.1
F32 = jnp.float32
BF16 = jnp.bfloat16


def fold(tile):
    return jnp.sum(tile.reshape(tile.shape[0] // 8, 8, tile.shape[1]), axis=0)


def kernel(
    side,
    n_sect,
    n_sec,
    coup_in,
    pairs_in,
    psi_one,
    psi_two,
    left,
    right,
    wave_one,
    wave_two,
    energies,
    env,
    renv,
    cand,
    come,
    own,
    sent,
    image,
    stat,
    stat_own,
    coef,
    parts,
    prev_wave,
    hop_one,
    hop_two,
    coup,
    pairs,
    load_sem,
    send_sem,
    recv_sem,
    relay_sem,
    stat_send,
    stat_recv,
    env_send,
    env_recv,
    hop_send,
    hop_recv,
    hand_send,
    hand_recv,
):
    sect = lax.axis_index("sect")
    me = lax.axis_index("sec")
    following = lax.rem(sect + 1, n_sect)
    previous = lax.rem(sect + n_sect - 1, n_sect)
    terms, held = left.shape[0], left.shape[1]
    near_terms = terms - hop_one.shape[0]
    column, row_at = lax.rem(sect, side), lax.div(sect, side)
    below = row_at * side + lax.rem(column + side - 1, side)
    above = row_at * side + lax.rem(column + 1, side)
    turns = lax.div(lax.rem(column + side - 2, side), side - 1)
    turned_from = lax.div(lax.rem(column + side - 1, side), side - 1)
    hop_to = turns * lax.rem(row_at + 1, side) * side + (1 - turns) * below
    hop_from = turned_from * (lax.rem(row_at + side - 1, side) * side + 1) + (1 - turned_from) * above
    half = n_sec // 2
    total = float(n_sec * held * BLK * BLK)

    def far_first(order):
        return lax.rem(held + (1 - 2 * lax.rem(order, 2)) * lax.div(order + 1, 2), held)

    barrier = pltpu.get_barrier_semaphore()

    def greet(step, _):
        peer = lax.rem(me + step, n_sec)
        pl.semaphore_signal(barrier, inc=1, device_id=(sect, peer), device_id_type=MESH)
        return 0

    lax.fori_loop(1, n_sec, greet, 0)
    for section in (following, previous, below, above, hop_to, hop_from):
        pl.semaphore_signal(barrier, inc=1, device_id=(section, me), device_id_type=MESH)

    def place(source, target, number):
        return pltpu.make_async_copy(source, target, load_sem.at[number])

    first = lax.rem(me, held)
    second = lax.rem(me + 1, held)
    loads = [
        place(psi_one, own.at[0], 0),
        place(psi_one.at[first], come.at[0, 2 * me], 1),
        place(psi_one.at[second], come.at[0, 2 * me + 1], 2),
        place(coup_in, coup, 8),
        place(pairs_in, pairs, 9),
        place(left, env.at[0], 3),
        place(right, renv, 4),
        place(psi_two, own.at[1], 5),
        place(psi_two.at[first], come.at[3, 2 * me], 6),
        place(psi_two.at[second], come.at[3, 2 * me + 1], 7),
    ]
    for load in loads:
        load.start()
    pl.semaphore_wait(barrier, n_sec + 5)

    def send_block(source, number, owner, kind, peer, done):
        pltpu.make_async_remote_copy(
            src_ref=source,
            dst_ref=come.at[number, 2 * owner + kind],
            send_sem=send_sem.at[number],
            recv_sem=done,
            device_id=(sect, peer),
            device_id_type=MESH,
        ).start()

    def send_sector(source, number, step):
        @pl.when(step != 1)
        def _():
            ahead = lax.rem(step + held - 1, held)
            send_block(source, number, me, 1, lax.rem(me + ahead, n_sec), relay_sem.at[number, ahead - 1])

        @pl.when(step != 0)
        def _():
            behind = held - step
            send_block(
                source, number, me, 0, lax.rem(me + n_sec - behind, n_sec), relay_sem.at[number, held - 2 + behind]
            )

        @pl.when(step == 0)
        def _():
            send_block(source, number, me, 1, lax.rem(me + n_sec - 1, n_sec), recv_sem.at[number])

        @pl.when(step == 1)
        def _():
            send_block(source, number, me, 0, lax.rem(me + 1, n_sec), recv_sem.at[number])

    def relay(number, between=None, low=0, high=None):
        def landed(lane):
            pltpu.make_async_copy(come.at[number, 0], come.at[number, 0], relay_sem.at[number, lane]).wait()

        def body(order, _):
            step = far_first(order)

            @pl.when(step != 1)
            def _():
                ahead = lax.rem(step + held - 1, held)
                owner = lax.rem(me + n_sec - ahead, n_sec)
                landed(ahead - 1)
                send_block(
                    come.at[number, 2 * owner + 1], number, owner, 0, lax.rem(me + 1, n_sec), recv_sem.at[number]
                )

            @pl.when(step != 0)
            def _():
                behind = held - step
                owner = lax.rem(me + behind, n_sec)
                landed(held - 2 + behind)
                send_block(
                    come.at[number, 2 * owner], number, owner, 1, lax.rem(me + n_sec - 1, n_sec), recv_sem.at[number]
                )

            if between is not None:
                pl.when(order == 1)(between)
            return 0

        lax.fori_loop(low, held if high is None else high, body, 0)

    def send_start(source, number, low, high):
        def body(order, _):
            step = far_first(order)
            send_sector(source.at[lax.rem(me + step, held)], number, step)
            return 0

        lax.fori_loop(low, high, body, 0)

    send_start(psi_one, 0, 0, held)

    def position(order):
        return lax.rem(me + far_first(order), held)

    near = pl.ds(0, near_terms)
    tail = pl.ds(near_terms, terms - near_terms)

    def near_env(order):
        return pltpu.make_async_remote_copy(
            src_ref=left.at[near, position(order)],
            dst_ref=env.at[1, near, position(order)],
            send_sem=env_send.at[order],
            recv_sem=env_recv.at[order],
            device_id=(following, me),
            device_id_type=MESH,
        )

    def hop(number):
        return pltpu.make_async_remote_copy(
            src_ref=(left.at[tail], hop_one, hop_two)[number],
            dst_ref=(hop_one, hop_two, env.at[1, tail])[number],
            send_sem=hop_send.at[number],
            recv_sem=hop_recv.at[number],
            device_id=(hop_to if number == 2 else below, me),
            device_id_type=MESH,
        )

    def pass_on(number):
        hop(number).wait_recv()
        hop(number + 1).start()

    hop(0).start()
    near_env(0).start()
    near_env(1).start()
    lanes = lax.broadcasted_iota(jnp.int32, (1, BLK), 1)
    blocks = pl.ds(0, 2 * n_sec - 2)
    relayed = pl.ds(0, 2 * held)

    def arrived(number):
        pltpu.make_async_copy(come.at[number, relayed], come.at[number, relayed], recv_sem.at[number]).wait()

    def left_here(number):
        pltpu.make_async_copy(come.at[number, blocks], come.at[number, blocks], send_sem.at[number]).wait()

    for load in loads:
        load.wait()
    relay(0)
    near_env(2).start()
    near_env(3).start()

    def begin(step):
        arrived(3 * step)

        def body(slot, _):
            cand[slot] = come[3 * step, slot]
            return 0

        lax.fori_loop(0, 2 * n_sec, body, 0, unroll=8)
        coef[2] = jnp.zeros((8, BLK), F32)

    def hand(local):
        return pltpu.make_async_remote_copy(
            src_ref=wave_one.at[local],
            dst_ref=prev_wave.at[local],
            send_sem=hand_send,
            recv_sem=hand_recv.at[local],
            device_id=(following, me),
            device_id_type=MESH,
        )

    def iterate(index, _):
        step = lax.div(index, ITERS)
        turn = lax.rem(index, ITERS)
        number = index + 1

        @pl.when(turn == 0)
        def _():
            begin(step)

        shift = coef[2, 0:1, :]

        def products(local):
            slots = []
            for pair in range(4):
                name = pairs[pair, local]
                slots.append(2 * lax.div(name, held) + lax.rem(name + n_sec - me, held))
            total_image = jnp.zeros((BLK, BLK), F32)
            for term in range(terms):
                mixed = None
                for pair in range(4):
                    part = coup[local, pair, term] * cand[slots[pair]].astype(F32)
                    mixed = part if mixed is None else mixed + part
                inner = jnp.dot(env[step, term, local], mixed.astype(BF16), preferred_element_type=F32)
                total_image = total_image + jnp.dot(
                    inner.astype(BF16), renv[term, local], preferred_element_type=F32
                )
            return total_image

        def sector(order, sums):
            turned = far_first(order)
            local = lax.rem(me + turned, held)

            @pl.when(index == ITERS)
            def _():
                hand(local).wait_recv()

                near_env(order).wait_recv()

                @pl.when(order == 0)
                def _():
                    hop(2).wait_recv()

                @pl.when(sect != 0)
                def _():
                    wave = prev_wave[local]
                    flipped = wave.astype(F32).T.astype(BF16)
                    for term in range(terms):
                        transit = jnp.dot(env[1, term, local], wave, preferred_element_type=F32)
                        passed = jnp.dot(flipped, transit.astype(BF16), preferred_element_type=F32)
                        env[1, term, local] = (passed * (1.0 / BLK)).astype(BF16)

                @pl.when(sect == 0)
                def _():
                    for term in range(terms):
                        env[1, term, local] = env[0, term, local]

            total_image = products(local)
            mine = own[step, local].astype(F32)
            rest = total_image - shift * mine

            sent[index, local] = rest.astype(BF16)

            @pl.when(turned < 2)
            def _():
                come[number, 2 * me + turned] = rest.astype(BF16)

            send_sector(sent.at[index, local], number, turned)
            square, cross, rests = sums
            return (square + fold(mine * mine), cross + fold(mine * rest), rests + fold(rest * rest))

        def last_sector(local, sums):
            mine = own[step, local].astype(F32)
            rest = products(local) - shift * mine
            image[local] = rest
            square, cross, rests = sums
            return (square + fold(mine * mine), cross + fold(mine * rest), rests + fold(rest * rest))

        zero = jnp.zeros((8, BLK), F32)

        def total_up(body, unroll):
            for kind, value in enumerate(lax.fori_loop(0, held, body, (zero, zero, zero), unroll=unroll)):
                parts[kind] = value

        @pl.when(turn < ITERS - 1)
        def _():
            total_up(sector, 1)

        @pl.when(turn == ITERS - 1)
        def _():
            total_up(last_sector, 4)

        row = None
        for kind in range(3):
            part = jnp.where(lanes == kind, jnp.sum(parts[kind], axis=(0, 1), keepdims=True), 0.0)
            row = part if row is None else row + part
        stat_own[index] = row
        stat[index, me] = row

        def tell(order, _):
            offset = half + (1 - 2 * lax.rem(order, 2)) * lax.div(order + 1, 2)
            pltpu.make_async_remote_copy(
                src_ref=stat_own.at[index],
                dst_ref=stat.at[index, me],
                send_sem=stat_send.at[index],
                recv_sem=stat_recv.at[index],
                device_id=(sect, lax.rem(me + offset, n_sec)),
                device_id_type=MESH,
            ).start()
            return 0

        lax.fori_loop(0, n_sec - 1, tell, 0)

        @pl.when(index == ITERS - 1)
        def _():
            relay(3, None, 0, 3)

        @pl.when(index == 0)
        def _():
            relay(number, functools.partial(pass_on, 0))
            near_env(4).start()
            near_env(5).start()
            send_start(psi_two, 3, 0, 2)

        @pl.when(index == 1)
        def _():
            relay(number, functools.partial(pass_on, 1))
            near_env(6).start()
            near_env(7).start()
            send_start(psi_two, 3, 2, held)

        @pl.when(index >= ITERS)
        def _():
            @pl.when(turn < ITERS - 1)
            def _():
                relay(number)

        others = pl.ds(0, n_sec - 1)
        pltpu.make_async_copy(stat.at[index, others], stat.at[index, others], stat_recv.at[index]).wait()
        table = jnp.sum(stat[index], axis=0)
        square, cross, rests = [
            jnp.broadcast_to(jnp.sum(jnp.where(lanes == kind, table, 0.0), axis=1, keepdims=True), (8, BLK))
            for kind in range(3)
        ]
        ratio = cross / square
        keep = 1.0 + DESCENT * ratio
        size = keep * keep * square - (2.0 * DESCENT) * keep * cross + (DESCENT * DESCENT) * rests
        scale = lax.rsqrt(size / total)
        coef[0] = keep * scale
        coef[1] = DESCENT * scale
        quot = coef[2] + ratio
        coef[2] = quot

        @pl.when(turn < ITERS - 1)
        def _():
            grow = coef[0, 0:1, :]
            drop = coef[1, 0:1, :]

            def own_body(local, _):
                own[step, local] = (
                    grow * own[step, local].astype(F32) - drop * sent[index, local].astype(F32)
                ).astype(BF16)
                return 0

            lax.fori_loop(0, held, own_body, 0, unroll=4)

            def renew(slot):
                cand[slot] = (
                    grow * cand[slot].astype(F32) - drop * come[number, slot].astype(F32)
                ).astype(BF16)

            renew(2 * me)
            renew(2 * me + 1)

            def direct(away, _):
                renew(2 * lax.rem(me + n_sec - away, n_sec) + 1)
                renew(2 * lax.rem(me + away, n_sec))
                return 0

            lax.fori_loop(1, held, direct, 0)
            arrived(number)

            def relayed_on(away, _):
                renew(2 * lax.rem(me + n_sec - away, n_sec))
                renew(2 * lax.rem(me + away, n_sec) + 1)
                return 0

            lax.fori_loop(1, held + 1, relayed_on, 0, unroll=4)

        def finish(wave, onward):
            grow = coef[0, 0:1, :]
            drop = coef[1, 0:1, :]

            def body(order, _):
                local = lax.rem(me + far_first(order), held)
                wave[local] = (grow * own[step, local].astype(F32) - drop * image[local]).astype(BF16)
                if onward:
                    hand(local).start()
                return 0

            lax.fori_loop(0, held, body, 0, unroll=1 if onward else 4)

        @pl.when(index == ITERS - 1)
        def _():
            finish(wave_one, True)
            energies[0:1, 0:1] = coef[2, 0:1, 0:1]
            relay(3, None, 3)

        @pl.when(index == 2 * ITERS - 1)
        def _():
            finish(wave_two, False)
            energies[0:1, 1:2] = coef[2, 0:1, 0:1]

        return 0

    lax.fori_loop(0, 2 * ITERS, iterate, 0)

    for number in (0, 1, 2, 3, 4, 5):
        left_here(number)

    def told(index, _):
        others = pl.ds(0, n_sec - 1)
        pltpu.make_async_copy(stat.at[index, others], stat.at[index, others], stat_send.at[index]).wait()
        return 0

    lax.fori_loop(0, 2 * ITERS, told, 0)

    for order in range(held):
        near_env(order).wait_send()
    for number in range(3):
        hop(number).wait_send()
    pltpu.make_async_copy(prev_wave, prev_wave, hand_send).wait()


def solution(mesh):
    n_sect, n_sec = mesh.shape["sect"], mesh.shape["sec"]
    side = int(round(n_sect**0.5))
    wide = P("sect", "sec", None, None)
    deep = P("sect", None, "sec", None, None)

    def on_device(psi_first, psi_second, left_env, right_env, couplings, pair_sector):
        terms, held = left_env.shape[1], left_env.shape[2]
        block = (BLK, BLK)
        hbm = pl.BlockSpec(memory_space=pltpu.HBM)
        far_terms = terms * 3 // 14
        vmem = pl.BlockSpec(memory_space=pltpu.VMEM)
        dma = pltpu.SemaphoreType.DMA
        waves = jax.ShapeDtypeStruct((held,) + block, BF16)
        one, two, energy = pl.pallas_call(
            functools.partial(kernel, side, n_sect, n_sec),
            out_shape=(waves, waves, jax.ShapeDtypeStruct((1, 2), F32)),
            in_specs=[hbm] * 6,
            out_specs=(vmem, vmem, vmem),
            scratch_shapes=[
                pltpu.VMEM((2, terms, held) + block, BF16),
                pltpu.VMEM((terms, held) + block, BF16),
                pltpu.VMEM((2 * n_sec,) + block, BF16),
                pltpu.VMEM((6, 2 * n_sec) + block, BF16),
                pltpu.VMEM((2, held) + block, BF16),
                pltpu.VMEM((6, held) + block, BF16),
                pltpu.VMEM((held,) + block, F32),
                pltpu.VMEM((6, n_sec, 1, BLK), F32),
                pltpu.VMEM((6, 1, BLK), F32),
                pltpu.VMEM((3, 8, BLK), F32),
                pltpu.VMEM((3, 8, BLK), F32),
                pltpu.VMEM((held,) + block, BF16),
                pltpu.VMEM((far_terms, held) + block, BF16),
                pltpu.VMEM((far_terms, held) + block, BF16),
                pltpu.SMEM(couplings.shape[1:], F32),
                pltpu.SMEM(pair_sector.shape[::-1], jnp.int32),
                dma((10,)),
                dma((6,)),
                dma((6,)),
                dma((6, 2 * held - 2)),
                dma((6,)),
                dma((6,)),
                dma((held,)),
                dma((held,)),
                dma((3,)),
                dma((3,)),
                dma,
                dma((held,)),
            ],
            compiler_params=pltpu.CompilerParams(
                collective_id=0, has_side_effects=True, vmem_limit_bytes=213 * 256 * 1024
            ),
        )(
            couplings[0],
            pair_sector.T,
            psi_first[0],
            psi_second[0],
            left_env[0],
            right_env[0],
        )
        return (one[None], two[None], energy)

    return jax.shard_map(
        on_device,
        mesh=mesh,
        in_specs=(wide, wide, deep, deep, wide, P("sec", None)),
        out_specs=(wide, wide, P("sect", None)),
        check_vma=False,
    )
```

```python
import functools

import jax
import jax.numpy as jnp
from jax import lax
from jax.experimental import pallas as pl
from jax.experimental.pallas import tpu as pltpu
from jax.sharding import PartitionSpec as P

MESH = pl.DeviceIdType.MESH
BLK = 128
ITERS = 3
DESCENT = 0.1
F32 = jnp.float32
BF16 = jnp.bfloat16


def fold(tile):
    return jnp.sum(tile.reshape(tile.shape[0] // 8, 8, tile.shape[1]), axis=0)


def kernel(
    side,
    n_sect,
    n_sec,
    coup_in,
    pairs_in,
    psi_one,
    psi_two,
    left,
    right,
    wave_one,
    wave_two,
    energies,
    env,
    renv,
    cand,
    come,
    own,
    sent,
    image,
    stat,
    stat_own,
    coef,
    parts,
    prev_wave,
    hop_one,
    hop_two,
    coup,
    pairs,
    load_sem,
    send_sem,
    recv_sem,
    relay_sem,
    stat_send,
    stat_recv,
    env_send,
    env_recv,
    hop_send,
    hop_recv,
    hand_send,
    hand_recv,
):
    sect = lax.axis_index("sect")
    me = lax.axis_index("sec")
    following = lax.rem(sect + 1, n_sect)
    previous = lax.rem(sect + n_sect - 1, n_sect)
    terms, held = left.shape[0], left.shape[1]
    near_terms = terms - hop_one.shape[0]
    column, row_at = lax.rem(sect, side), lax.div(sect, side)
    below = row_at * side + lax.rem(column + side - 1, side)
    above = row_at * side + lax.rem(column + 1, side)
    turns = lax.div(lax.rem(column + side - 2, side), side - 1)
    turned_from = lax.div(lax.rem(column + side - 1, side), side - 1)
    hop_to = turns * lax.rem(row_at + 1, side) * side + (1 - turns) * below
    hop_from = turned_from * (lax.rem(row_at + side - 1, side) * side + 1) + (1 - turned_from) * above
    half = n_sec // 2
    total = float(n_sec * held * BLK * BLK)

    def far_first(order):
        return lax.rem(held + (1 - 2 * lax.rem(order, 2)) * lax.div(order + 1, 2), held)

    barrier = pltpu.get_barrier_semaphore()

    def greet(step, _):
        peer = lax.rem(me + step, n_sec)
        pl.semaphore_signal(barrier, inc=1, device_id=(sect, peer), device_id_type=MESH)
        return 0

    lax.fori_loop(1, n_sec, greet, 0)
    for section in (following, previous, below, above, hop_to, hop_from):
        pl.semaphore_signal(barrier, inc=1, device_id=(section, me), device_id_type=MESH)

    def place(source, target, number):
        return pltpu.make_async_copy(source, target, load_sem.at[number])

    first = lax.rem(me, held)
    second = lax.rem(me + 1, held)
    loads = [
        place(psi_one, own.at[0], 0),
        place(psi_one.at[first], come.at[0, 2 * me], 1),
        place(psi_one.at[second], come.at[0, 2 * me + 1], 2),
        place(coup_in, coup, 8),
        place(pairs_in, pairs, 9),
        place(left, env.at[0], 3),
        place(right, renv, 4),
        place(psi_two, own.at[1], 5),
        place(psi_two.at[first], come.at[3, 2 * me], 6),
        place(psi_two.at[second], come.at[3, 2 * me + 1], 7),
    ]
    for load in loads:
        load.start()
    pl.semaphore_wait(barrier, n_sec + 5)

    def send_block(source, number, owner, kind, peer, done):
        pltpu.make_async_remote_copy(
            src_ref=source,
            dst_ref=come.at[number, 2 * owner + kind],
            send_sem=send_sem.at[number],
            recv_sem=done,
            device_id=(sect, peer),
            device_id_type=MESH,
        ).start()

    def send_sector(source, number, step):
        @pl.when(step != 1)
        def _():
            ahead = lax.rem(step + held - 1, held)
            send_block(source, number, me, 1, lax.rem(me + ahead, n_sec), relay_sem.at[number, ahead - 1])

        @pl.when(step != 0)
        def _():
            behind = held - step
            send_block(
                source, number, me, 0, lax.rem(me + n_sec - behind, n_sec), relay_sem.at[number, held - 2 + behind]
            )

        @pl.when(step == 0)
        def _():
            send_block(source, number, me, 1, lax.rem(me + n_sec - 1, n_sec), recv_sem.at[number])

        @pl.when(step == 1)
        def _():
            send_block(source, number, me, 0, lax.rem(me + 1, n_sec), recv_sem.at[number])

    def relay(number, between=None, low=0, high=None):
        def landed(lane):
            pltpu.make_async_copy(come.at[number, 0], come.at[number, 0], relay_sem.at[number, lane]).wait()

        def body(order, _):
            step = far_first(order)

            @pl.when(step != 1)
            def _():
                ahead = lax.rem(step + held - 1, held)
                owner = lax.rem(me + n_sec - ahead, n_sec)
                landed(ahead - 1)
                send_block(
                    come.at[number, 2 * owner + 1], number, owner, 0, lax.rem(me + 1, n_sec), recv_sem.at[number]
                )

            @pl.when(step != 0)
            def _():
                behind = held - step
                owner = lax.rem(me + behind, n_sec)
                landed(held - 2 + behind)
                send_block(
                    come.at[number, 2 * owner], number, owner, 1, lax.rem(me + n_sec - 1, n_sec), recv_sem.at[number]
                )

            if between is not None:
                pl.when(order == 1)(between)
            return 0

        lax.fori_loop(low, held if high is None else high, body, 0)

    def send_start(source, number, low, high):
        def body(order, _):
            step = far_first(order)
            send_sector(source.at[lax.rem(me + step, held)], number, step)
            return 0

        lax.fori_loop(low, high, body, 0)

    send_start(psi_one, 0, 0, held)

    def position(order):
        return lax.rem(me + far_first(order), held)

    near = pl.ds(0, near_terms)
    tail = pl.ds(near_terms, terms - near_terms)

    def near_env(order):
        return pltpu.make_async_remote_copy(
            src_ref=left.at[near, position(order)],
            dst_ref=env.at[1, near, position(order)],
            send_sem=env_send.at[order],
            recv_sem=env_recv.at[order],
            device_id=(following, me),
            device_id_type=MESH,
        )

    def hop(number):
        return pltpu.make_async_remote_copy(
            src_ref=(left.at[tail], hop_one, hop_two)[number],
            dst_ref=(hop_one, hop_two, env.at[1, tail])[number],
            send_sem=hop_send.at[number],
            recv_sem=hop_recv.at[number],
            device_id=(hop_to if number == 2 else below, me),
            device_id_type=MESH,
        )

    def pass_on(number):
        hop(number).wait_recv()
        hop(number + 1).start()

    hop(0).start()
    near_env(0).start()
    near_env(1).start()
    lanes = lax.broadcasted_iota(jnp.int32, (1, BLK), 1)
    blocks = pl.ds(0, 2 * n_sec - 2)
    relayed = pl.ds(0, 2 * held)

    def arrived(number):
        pltpu.make_async_copy(come.at[number, relayed], come.at[number, relayed], recv_sem.at[number]).wait()

    def left_here(number):
        pltpu.make_async_copy(come.at[number, blocks], come.at[number, blocks], send_sem.at[number]).wait()

    for load in loads:
        load.wait()
    relay(0)
    near_env(2).start()
    near_env(3).start()

    def begin(step):
        arrived(3 * step)

        def body(slot, _):
            cand[slot] = come[3 * step, slot]
            return 0

        lax.fori_loop(0, 2 * n_sec, body, 0, unroll=8)
        coef[2] = jnp.zeros((8, BLK), F32)

    def hand(local):
        return pltpu.make_async_remote_copy(
            src_ref=wave_one.at[local],
            dst_ref=prev_wave.at[local],
            send_sem=hand_send,
            recv_sem=hand_recv.at[local],
            device_id=(following, me),
            device_id_type=MESH,
        )

    def iterate(index, _):
        step = lax.div(index, ITERS)
        turn = lax.rem(index, ITERS)
        number = index + 1

        @pl.when(turn == 0)
        def _():
            begin(step)

        shift = coef[2, 0:1, :]

        def products(local):
            slots = []
            for pair in range(4):
                name = pairs[pair, local]
                slots.append(2 * lax.div(name, held) + lax.rem(name + n_sec - me, held))
            total_image = jnp.zeros((BLK, BLK), F32)
            for term in range(terms):
                mixed = None
                for pair in range(4):
                    part = coup[local, pair, term] * cand[slots[pair]].astype(F32)
                    mixed = part if mixed is None else mixed + part
                inner = jnp.dot(env[step, term, local], mixed.astype(BF16), preferred_element_type=F32)
                total_image = total_image + jnp.dot(
                    inner.astype(BF16), renv[term, local], preferred_element_type=F32
                )
            return total_image

        def sector(order, sums):
            turned = far_first(order)
            local = lax.rem(me + turned, held)

            @pl.when(index == ITERS)
            def _():
                hand(local).wait_recv()

                near_env(order).wait_recv()

                @pl.when(order == 0)
                def _():
                    hop(2).wait_recv()

                @pl.when(sect != 0)
                def _():
                    wave = prev_wave[local]
                    flipped = wave.astype(F32).T.astype(BF16)
                    for term in range(terms):
                        transit = jnp.dot(env[1, term, local], wave, preferred_element_type=F32)
                        passed = jnp.dot(flipped, transit.astype(BF16), preferred_element_type=F32)
                        env[1, term, local] = (passed * (1.0 / BLK)).astype(BF16)

                @pl.when(sect == 0)
                def _():
                    for term in range(terms):
                        env[1, term, local] = env[0, term, local]

            total_image = products(local)
            mine = own[step, local].astype(F32)
            rest = total_image - shift * mine

            sent[index, local] = rest.astype(BF16)

            @pl.when(turned < 2)
            def _():
                come[number, 2 * me + turned] = rest.astype(BF16)

            send_sector(sent.at[index, local], number, turned)
            square, cross, rests = sums
            return (square + fold(mine * mine), cross + fold(mine * rest), rests + fold(rest * rest))

        def last_sector(local, sums):
            mine = own[step, local].astype(F32)
            rest = products(local) - shift * mine
            image[local] = rest
            square, cross, rests = sums
            return (square + fold(mine * mine), cross + fold(mine * rest), rests + fold(rest * rest))

        zero = jnp.zeros((8, BLK), F32)

        def total_up(body, unroll):
            for kind, value in enumerate(lax.fori_loop(0, held, body, (zero, zero, zero), unroll=unroll)):
                parts[kind] = value

        @pl.when(turn < ITERS - 1)
        def _():
            total_up(sector, 1)

        @pl.when(turn == ITERS - 1)
        def _():
            total_up(last_sector, 4)

        row = None
        for kind in range(3):
            part = jnp.where(lanes == kind, jnp.sum(parts[kind], axis=(0, 1), keepdims=True), 0.0)
            row = part if row is None else row + part
        stat_own[index] = row
        stat[index, me] = row

        def tell(order, _):
            offset = half + (1 - 2 * lax.rem(order, 2)) * lax.div(order + 1, 2)
            pltpu.make_async_remote_copy(
                src_ref=stat_own.at[index],
                dst_ref=stat.at[index, me],
                send_sem=stat_send.at[index],
                recv_sem=stat_recv.at[index],
                device_id=(sect, lax.rem(me + offset, n_sec)),
                device_id_type=MESH,
            ).start()
            return 0

        lax.fori_loop(0, n_sec - 1, tell, 0)

        @pl.when(index == ITERS - 1)
        def _():
            relay(3, None, 0, 3)

        @pl.when(index == 0)
        def _():
            relay(number, functools.partial(pass_on, 0))
            near_env(4).start()
            near_env(5).start()
            send_start(psi_two, 3, 0, 2)

        @pl.when(index == 1)
        def _():
            relay(number, functools.partial(pass_on, 1))
            near_env(6).start()
            near_env(7).start()

        @pl.when(index >= ITERS)
        def _():
            @pl.when(turn < ITERS - 1)
            def _():
                relay(number)

        others = pl.ds(0, n_sec - 1)
        pltpu.make_async_copy(stat.at[index, others], stat.at[index, others], stat_recv.at[index]).wait()
        table = jnp.sum(stat[index], axis=0)
        square, cross, rests = [
            jnp.broadcast_to(jnp.sum(jnp.where(lanes == kind, table, 0.0), axis=1, keepdims=True), (8, BLK))
            for kind in range(3)
        ]
        ratio = cross / square
        keep = 1.0 + DESCENT * ratio
        size = keep * keep * square - (2.0 * DESCENT) * keep * cross + (DESCENT * DESCENT) * rests
        scale = lax.rsqrt(size / total)
        coef[0] = keep * scale
        coef[1] = DESCENT * scale
        quot = coef[2] + ratio
        coef[2] = quot

        @pl.when(turn < ITERS - 1)
        def _():
            grow = coef[0, 0:1, :]
            drop = coef[1, 0:1, :]

            def own_body(local, _):
                own[step, local] = (
                    grow * own[step, local].astype(F32) - drop * sent[index, local].astype(F32)
                ).astype(BF16)
                return 0

            lax.fori_loop(0, held, own_body, 0, unroll=4)

            def renew(slot):
                cand[slot] = (
                    grow * cand[slot].astype(F32) - drop * come[number, slot].astype(F32)
                ).astype(BF16)

            renew(2 * me)
            renew(2 * me + 1)

            def direct(away, _):
                renew(2 * lax.rem(me + n_sec - away, n_sec) + 1)
                renew(2 * lax.rem(me + away, n_sec))
                return 0

            lax.fori_loop(1, held, direct, 0)

            @pl.when(index == 1)
            def _():
                send_start(psi_two, 3, 2, held)

            arrived(number)

            def relayed_on(away, _):
                renew(2 * lax.rem(me + n_sec - away, n_sec))
                renew(2 * lax.rem(me + away, n_sec) + 1)
                return 0

            lax.fori_loop(1, held + 1, relayed_on, 0, unroll=4)

        def finish(wave, onward):
            grow = coef[0, 0:1, :]
            drop = coef[1, 0:1, :]

            def body(order, _):
                local = lax.rem(me + far_first(order), held)
                wave[local] = (grow * own[step, local].astype(F32) - drop * image[local]).astype(BF16)
                if onward:
                    hand(local).start()
                return 0

            lax.fori_loop(0, held, body, 0, unroll=1 if onward else 4)

        @pl.when(index == ITERS - 1)
        def _():
            finish(wave_one, True)
            energies[0:1, 0:1] = coef[2, 0:1, 0:1]
            relay(3, None, 3)

        @pl.when(index == 2 * ITERS - 1)
        def _():
            finish(wave_two, False)
            energies[0:1, 1:2] = coef[2, 0:1, 0:1]

        return 0

    lax.fori_loop(0, 2 * ITERS, iterate, 0)

    for number in (0, 1, 2, 3, 4, 5):
        left_here(number)

    def told(index, _):
        others = pl.ds(0, n_sec - 1)
        pltpu.make_async_copy(stat.at[index, others], stat.at[index, others], stat_send.at[index]).wait()
        return 0

    lax.fori_loop(0, 2 * ITERS, told, 0)

    for order in range(held):
        near_env(order).wait_send()
    for number in range(3):
        hop(number).wait_send()
    pltpu.make_async_copy(prev_wave, prev_wave, hand_send).wait()


def solution(mesh):
    n_sect, n_sec = mesh.shape["sect"], mesh.shape["sec"]
    side = int(round(n_sect**0.5))
    wide = P("sect", "sec", None, None)
    deep = P("sect", None, "sec", None, None)

    def on_device(psi_first, psi_second, left_env, right_env, couplings, pair_sector):
        terms, held = left_env.shape[1], left_env.shape[2]
        block = (BLK, BLK)
        hbm = pl.BlockSpec(memory_space=pltpu.HBM)
        far_terms = terms * 3 // 14
        vmem = pl.BlockSpec(memory_space=pltpu.VMEM)
        dma = pltpu.SemaphoreType.DMA
        waves = jax.ShapeDtypeStruct((held,) + block, BF16)
        one, two, energy = pl.pallas_call(
            functools.partial(kernel, side, n_sect, n_sec),
            out_shape=(waves, waves, jax.ShapeDtypeStruct((1, 2), F32)),
            in_specs=[hbm] * 6,
            out_specs=(vmem, vmem, vmem),
            scratch_shapes=[
                pltpu.VMEM((2, terms, held) + block, BF16),
                pltpu.VMEM((terms, held) + block, BF16),
                pltpu.VMEM((2 * n_sec,) + block, BF16),
                pltpu.VMEM((6, 2 * n_sec) + block, BF16),
                pltpu.VMEM((2, held) + block, BF16),
                pltpu.VMEM((6, held) + block, BF16),
                pltpu.VMEM((held,) + block, F32),
                pltpu.VMEM((6, n_sec, 1, BLK), F32),
                pltpu.VMEM((6, 1, BLK), F32),
                pltpu.VMEM((3, 8, BLK), F32),
                pltpu.VMEM((3, 8, BLK), F32),
                pltpu.VMEM((held,) + block, BF16),
                pltpu.VMEM((far_terms, held) + block, BF16),
                pltpu.VMEM((far_terms, held) + block, BF16),
                pltpu.SMEM(couplings.shape[1:], F32),
                pltpu.SMEM(pair_sector.shape[::-1], jnp.int32),
                dma((10,)),
                dma((6,)),
                dma((6,)),
                dma((6, 2 * held - 2)),
                dma((6,)),
                dma((6,)),
                dma((held,)),
                dma((held,)),
                dma((3,)),
                dma((3,)),
                dma,
                dma((held,)),
            ],
            compiler_params=pltpu.CompilerParams(
                collective_id=0, has_side_effects=True, vmem_limit_bytes=213 * 256 * 1024
            ),
        )(
            couplings[0],
            pair_sector.T,
            psi_first[0],
            psi_second[0],
            left_env[0],
            right_env[0],
        )
        return (one[None], two[None], energy)

    return jax.shard_map(
        on_device,
        mesh=mesh,
        in_specs=(wide, wide, deep, deep, wide, P("sec", None)),
        out_specs=(wide, wide, P("sect", None)),
        check_vma=False,
    )
```
